512 devices in a mesh: tm: 128 (over z, x, y_lo), tile: 4 (over y_hi, core).
Axes of the slice: x: 4, y: 4 (y_hi: 2, y_lo: 2; y = y_hi * 2 + y_lo), z: 16, core: 2. Of those that a mesh axis runs over, the one named last changes fastest.
Arguments:
- operator: float32 [128, 768, 768], P('tm', 'tile'), may hold values from -4 to 20, as said below
- initial: float32 [128, 768, 768], P('tm', 'tile'), may hold values from -1 to 2, as said below
- block_sizes: int32 [128], P('tm'), may hold values from 512 to 768, as said below
- link_index: int32 [128, 512], P('tm'), may hold values from 0 to 511, as said below
- link_pair: bfloat16 [128, 768, 512], P('tm', 'tile'), may hold values from -0.4375 to 0.4375
- link_global: bfloat16 [128, 768, 512], P('tm', 'tile'), may hold values from -0.109375 to 0.109375
- schur_base: float32 [512, 512], P('tile'), may hold values from -4 to 20, as said below
- schur_start: float32 [512, 512], P('tile'), may hold values from -1 to 2, as said below
Outputs:
- link_diag: float32 [128, 256, 256], P('tm', 'tile')
- link_off: float32 [128, 256, 256], P('tm', 'tile')
- link_cross: float32 [128, 256, 512], P('tm', 'tile')
- global_schur: float32 [512, 512], P('tile')
- back_cols: float32 [128, 768, 512], P('tm', 'tile')
The draws below stay inside these ranges and needn't reach their ends.
Inputs may be any that keep to these rules, and one draw needn't show every extreme that they name: `operator`: symmetric. `initial`: symmetric. `schur_base`: symmetric. `schur_start`: symmetric. `block_sizes`: some block has 768 live variables and some has 512. `link_index`: each row is a permutation of 0 to 511 that keeps every index j within its group of 128, j // 128.
All inputs are finite; a program needn't handle non-finite values.
Results may differ from the reference program's by a relative error of at most 0.0003.
Values may be sent and summed in bfloat16 or wider, within the bound.
A program may use at most 64 MiB of HBM per device.

```python
import jax
import jax.numpy as jnp
from jax import lax

NB = 768
LINK = 256
GLINK = 512
STEPS = 2
TIMES = 128
OWN = 128


def spread_scales(key, count, size):
    upper = jnp.log(10.0)
    return jnp.exp(jax.random.uniform(jax.random.fold_in(key, 7), (count, size), jnp.float32, 0.0, upper))


def symmetric_noise(key, count, size, strength):
    raw = jax.random.normal(key, (count, size, size), jnp.float32)
    both = (raw + jnp.swapaxes(raw, 1, 2)) * 0.70710678
    return both * (strength / size ** 0.5)


def scaled_pair(key, count, size, strength, invert):
    scales = spread_scales(key, count, size)
    noise = symmetric_noise(key, count, size, strength)
    unit = jnp.eye(size, dtype=jnp.float32)[None]
    roots = jnp.sqrt(scales)
    if invert:
        roots = 1.0 / roots
    return roots[:, :, None] * (unit + noise) * roots[:, None, :]


def draw_operator(key, part):
    return scaled_pair(jax.random.fold_in(key, 21), TIMES, NB, 0.2, False)


def draw_initial(key, part):
    base = jax.random.fold_in(key, 21)
    scales_key = base
    noise = symmetric_noise(jax.random.fold_in(key, 31), TIMES, NB, 0.1)
    roots = 1.0 / jnp.sqrt(spread_scales(scales_key, TIMES, NB))
    unit = jnp.eye(NB, dtype=jnp.float32)[None]
    return roots[:, :, None] * (unit + noise) * roots[:, None, :]


def draw_schur_base(key, part):
    return scaled_pair(jax.random.fold_in(key, 41), 1, GLINK, 0.2, False)[0]


def draw_schur_start(key, part):
    base = jax.random.fold_in(key, 41)
    noise = symmetric_noise(jax.random.fold_in(key, 51), 1, GLINK, 0.1)
    roots = 1.0 / jnp.sqrt(spread_scales(base, 1, GLINK))
    unit = jnp.eye(GLINK, dtype=jnp.float32)[None]
    return (roots[:, :, None] * (unit + noise) * roots[:, None, :])[0]


def draw_block_sizes(key, part):
    lowest = NB * 2 // 3
    values = jax.random.randint(jax.random.fold_in(key, 61), (TIMES,), lowest, NB + 1)
    high_pos = jax.random.randint(jax.random.fold_in(key, 62), (), 0, TIMES)
    low_pos = (high_pos + 1 + jax.random.randint(jax.random.fold_in(key, 63), (), 0, TIMES - 1)) % TIMES
    values = values.at[high_pos].set(NB)
    values = values.at[low_pos].set(lowest)
    return values.astype(jnp.int32)


def draw_link_index(key, part):
    groups = GLINK // OWN
    keys = jax.random.split(jax.random.fold_in(key, 71), TIMES * groups)
    perms = jax.vmap(lambda single: jax.random.permutation(single, OWN))(keys)
    perms = perms.reshape(TIMES, groups, OWN).astype(jnp.int32)
    offsets = (jnp.arange(groups, dtype=jnp.int32) * OWN)[None, :, None]
    return (perms + offsets).reshape(TIMES, GLINK).astype(jnp.int32)


def with_spikes(entries, stream_key, source, target, parts, factor):
    owner, partner = [(jnp.arange(entries.shape[position]) // (entries.shape[position] // parts)).reshape([-1 if axis == position else 1 for axis in range(entries.ndim)]) for position in (source, target)]
    chosen = jax.random.permutation(stream_key, parts)[partner]
    strong = (owner == chosen) | (owner == (partner + parts // 2) % parts)
    return jnp.where(strong, factor * entries, entries)


def block_levels(own_key, dims, shards, smallest, largest):
    gain = 1.0
    for position, blocks in shards:
        steps = jax.random.uniform(jax.random.fold_in(jax.random.fold_in(own_key, 6), position), (blocks,), jnp.float32, smallest / len(shards), largest / len(shards))
        gain = gain * jnp.repeat(jnp.exp(steps), dims[position] // blocks).reshape((-1,) + (1,) * (len(dims) - 1 - position))
    return gain


def gaussian(rng, extent, scale, bound, cuts=(), held_as=jnp.bfloat16):
    gain = block_levels(rng, extent, cuts, -0.22, 0.18) if cuts else 1.0
    entries = jax.random.normal(rng, extent, jnp.float32) * scale * gain
    return jnp.minimum(jnp.maximum(entries, -bound), bound).astype(held_as)


def bell_draw_with(own_key, extent, deviation, limit, shards, heavy, held_as=jnp.bfloat16):
    values = deviation * jax.random.normal(own_key, extent, jnp.float32)
    if shards:
        values = values * block_levels(own_key, extent, shards, -0.22, 0.18)
    return jnp.clip(with_spikes(values, jax.random.fold_in(own_key, 3), *heavy), -limit, limit).astype(held_as)


def setup_inputs(seed: int = 0) -> dict:
    streams_of = jax.random.split(jax.random.key(seed), 9)
    return {
        "operator": draw_operator(jax.random.fold_in(streams_of[8], 71), 0),
        "initial": draw_initial(jax.random.fold_in(streams_of[8], 71), 0),
        "block_sizes": draw_block_sizes(jax.random.fold_in(streams_of[8], 71), 0),
        "link_index": draw_link_index(jax.random.fold_in(streams_of[8], 71), 0),
        "link_pair": gaussian(streams_of[4], (TIMES, NB, 2 * LINK), (NB // 4) ** -0.5, 0.4375, ((0, 128), (1, 4))),
        "link_global": bell_draw_with(streams_of[5], (TIMES, NB, GLINK), (1.5 / (NB * TIMES) ** 0.5), 0.109375, ((0, 128), (1, 4)), (0, 2, 128, 5.5)),
        "schur_base": draw_schur_base(jax.random.fold_in(streams_of[8], 71), 0),
        "schur_start": draw_schur_start(jax.random.fold_in(streams_of[8], 71), 0),
    }


HIGH = lax.Precision.HIGHEST


def matmul(left_side, right_side):
    return jnp.dot(left_side, right_side, precision=HIGH, preferred_element_type=jnp.float32)


def block_terms(inputs):
    op_block, init_block, pair_block, glob_block, size_value, index_row = inputs
    block_order = op_block.shape[0]
    ids = jnp.arange(block_order, dtype=jnp.int32)
    live = (ids < size_value).astype(jnp.float32)
    unit = jnp.eye(block_order, dtype=jnp.float32)

    def effective(matrix):
        return matrix * live[:, None] * live[None, :] + unit * (1.0 - live)[:, None]

    kmatrix = effective(op_block)
    xmatrix = effective(init_block)
    for step in range(STEPS):
        xmatrix = 2.0 * xmatrix - matmul(matmul(xmatrix, kmatrix), xmatrix)
    pair_live = pair_block.astype(jnp.float32) * live[:, None]
    glob_live = jnp.take(glob_block.astype(jnp.float32), index_row, axis=1) * live[:, None]
    solved = matmul(xmatrix, jnp.concatenate([pair_live, glob_live], axis=1))
    e_part = pair_live[:, :LINK]
    f_part = pair_live[:, LINK:]
    y_e = solved[:, :LINK]
    y_f = solved[:, LINK:2 * LINK]
    y_g = solved[:, 2 * LINK:]

    def inner(left_side, right_side):
        return matmul(left_side.T, right_side)

    return (inner(f_part, y_f), inner(e_part, y_e), inner(e_part, y_f), inner(e_part, y_g),
            inner(f_part, y_g), inner(glob_live, y_g), y_g)


def reference(operator, initial, block_sizes, link_index, link_pair, link_global, schur_base, schur_start):
    terms = lax.map(block_terms, (operator, initial, link_pair, link_global, block_sizes, link_index))
    f_diag, e_diag, e_off, e_cross, f_cross, g_terms, y_glob = terms
    e_next = jnp.concatenate([e_diag[1:], jnp.zeros_like(e_diag[:1])], axis=0)
    c_next = jnp.concatenate([e_cross[1:], jnp.zeros_like(e_cross[:1])], axis=0)
    link_diag = f_diag + e_next
    link_cross = f_cross + c_next
    global_schur = schur_base + jnp.sum(g_terms, axis=0)
    inverse = 2.0 * schur_start - matmul(matmul(schur_start, global_schur), schur_start)
    back_cols = jnp.einsum("tij,jk->tik", y_glob, inverse, precision=HIGH)
    return link_diag, e_off, link_cross, global_schur, back_cols
```

```python
import functools

import jax
import jax.numpy as jnp
from jax import lax
from jax.experimental import pallas as pl
from jax.experimental.pallas import tpu as pltpu
from jax.sharding import PartitionSpec as P

MESH = pl.DeviceIdType.MESH
BF = jnp.bfloat16
F32 = jnp.float32
PLANE = 8
HALF = 384
ROWS = 192


def al(value, step):
    return pl.multiple_of(value, step)


def dot(left, right):
    return jnp.dot(left, right, preferred_element_type=F32)


def dot_nt(left, right):
    return lax.dot_general(left, right, (((1,), (1,)), ((), ())), preferred_element_type=F32)


def split(value):
    high = value.astype(BF)
    return high, (value - high.astype(F32)).astype(BF)


def product(value, high, low):
    value_high, value_low = split(value)
    return dot(value_high, high) + dot(value_high, low) + dot(value_low, high)


def position():
    tm = lax.axis_index("tm")
    ti = lax.axis_index("tile")
    h = ti // 2
    return tm, ti, h, ti - 2 * h


def remote(src, dst, send, recv, device):
    return pltpu.make_async_remote_copy(
        src_ref=src, dst_ref=dst, send_sem=send, recv_sem=recv, device_id=device, device_id_type=MESH
    )


def greet(devices):
    barrier = pltpu.get_barrier_semaphore()
    for device in devices:
        pl.semaphore_signal(barrier, inc=1, device_id=device, device_id_type=MESH)


def place_ids(h, first, count, axis, shape):
    ids = lax.broadcasted_iota(jnp.int32, shape, axis) + first
    return jnp.where(ids < HALF, ids + h * HALF, ids - h * HALF)


def gather_kernel(
    sizes, k_hbm, x_hbm, g_hbm,
    xh, xl, kh, kl, g_out,
    rows_x, rows_k, diag_x, diag_k, rows_g,
    local_sem, send_sem, recv_sem,
):
    tm, ti, h, c = position()
    mate = (tm, ti + 1 - 2 * c)
    cross = (tm, lax.rem(ti + 2, 4))
    size = sizes[0]
    greet((mate, cross))
    pl.semaphore_wait(pltpu.get_barrier_semaphore(), 2)
    own = al(h * HALF, 128)
    oth = al(HALF - h * HALF, 128)
    slots = [0]

    def slot():
        slots[0] += 1
        return slots[0] - 1

    def copy(src, dst, device):
        at = slot()
        made = remote(src, dst, send_sem.at[at], recv_sem.at[at], device)
        made.start()
        return made

    def pieces(ref):
        return [
            ref.at[pl.ds(al(256 * c, 128), 128), pl.ds(al(256 * c, 128), 128)],
            ref.at[pl.ds(al(256 * c, 128), 128), pl.ds(al(128 - 128 * c, 128), 128)],
            ref.at[pl.ds(al(128 + 64 * c, 64), 64), pl.ds(128, 256)],
        ]

    def other_pieces(ref):
        return pieces(ref)

    def sources(hbm):
        return [
            hbm.at[pl.ds(al(64 * c, 64), 128), pl.ds(al(own + 256 * c, 128), 128)],
            hbm.at[pl.ds(al(64 * c, 64), 128), pl.ds(al(own + 128 - 128 * c, 128), 128)],
            hbm.at[pl.ds(al(128 - 128 * c, 64), 64), pl.ds(al(own + 128, 128), 256)],
        ]

    mine = pl.ds(al(ROWS * c, 64), ROWS)
    far = pl.ds(al(HALF + ROWS * c, 64), ROWS)
    cross_x = [copy(a, b, cross) for a, b in zip(sources(x_hbm), pieces(diag_x))]
    cross_k = [copy(a, b, cross) for a, b in zip(sources(k_hbm), pieces(diag_k))]
    cross_g = copy(g_hbm, rows_g.at[far], cross)

    def halves(hbm, rows):
        return [
            (hbm.at[:, pl.ds(own, HALF)], rows.at[mine, pl.ds(0, HALF)]),
            (hbm.at[:, pl.ds(oth, HALF)], rows.at[mine, pl.ds(HALF, HALF)]),
        ]

    mate_x = [copy(a, b, mate) for a, b in halves(x_hbm, rows_x)]
    mate_k = [copy(a, b, mate) for a, b in halves(k_hbm, rows_k)]
    mate_g = copy(g_hbm, rows_g.at[mine], mate)
    local = []
    for a, b in halves(x_hbm, rows_x) + halves(k_hbm, rows_k) + [(g_hbm, rows_g.at[mine])]:
        made = pltpu.make_async_copy(a, b, local_sem.at[len(local)])
        made.start()
        local.append(made)

    def effective(block, first_row, first_col):
        row = place_ids(h, first_row, 0, 0, block.shape)
        col = place_ids(h, first_col, 0, 1, block.shape)
        unit = jnp.where(row == col, 1.0, 0.0).astype(F32)
        return jnp.where((row < size) & (col < size), block, unit)

    def store(high, low, row, col, value):
        n, m = value.shape
        value_high, value_low = split(value)
        high[pl.ds(row, n), pl.ds(col, m)] = value_high
        low[pl.ds(row, n), pl.ds(col, m)] = value_low

    def own_rows(rows, high, low):
        for i in range(3):
            at = 128 * i
            store(high, low, at, 0, effective(rows[pl.ds(at, 128), pl.ds(0, HALF)], at, 0))
            block = effective(rows[pl.ds(at, 128), pl.ds(HALF, HALF)], at, HALF)
            store(high, low, at, HALF, block)
            store(high, low, HALF, at, block.T)

    def far_rows(diag, high, low):
        for i in range(3):
            j, k = (i + 1) % 3, (i + 2) % 3
            at = HALF + 128 * i
            for col, block in (
                (i, diag[pl.ds(128 * i, 128), pl.ds(128 * i, 128)]),
                (j, diag[pl.ds(128 * i, 128), pl.ds(128 * j, 128)]),
            ):
                block = effective(block, at, HALF + 128 * col)
                store(high, low, at, HALF + 128 * col, block)
                if col == j:
                    store(high, low, HALF + 128 * j, at, block.T)

    def hand_on(came, refs):
        passed = []
        for made, ref in zip(came, refs):
            made.wait_recv()
            passed.append(copy(ref, ref, mate))
        return passed

    local[0].wait()
    local[1].wait()
    for made in mate_x:
        made.wait_recv()
    own_rows(rows_x, xh, xl)
    passed_x = hand_on(cross_x, pieces(diag_x))
    local[2].wait()
    local[3].wait()
    for made in mate_k:
        made.wait_recv()
    own_rows(rows_k, kh, kl)
    for made in passed_x:
        made.wait_recv()
    far_rows(diag_x, xh, xl)
    passed_k = hand_on(cross_k, pieces(diag_k))
    for made in passed_k:
        made.wait_recv()
    far_rows(diag_k, kh, kl)
    local[4].wait()
    mate_g.wait_recv()
    passed_g = hand_on([cross_g], [rows_g.at[far]])
    passed_g[0].wait_recv()
    row = place_ids(h, 0, 0, 0, rows_g.shape)
    g_out[...] = jnp.where(row < size, rows_g[...].astype(F32), 0.0).astype(BF)
    for made in cross_x + cross_k + [cross_g] + mate_x + mate_k + [mate_g] + passed_x + passed_k + passed_g:
        made.wait_send()


def reduce_kernel(
    z_count,
    sizes, index, xh, xl, kh, kl, g, base, pair_hbm, start_hbm,
    diag_out, off_out, cross_out, schur_out, back_out,
    g_perm, panel, came_a, piece, came_z, schur, pair, near, nxt, nxt_came, start_f, yg, wide,
    s_high, s_low, t_high, t_low,
    local_sem, send_a, recv_a, send_z, recv_z, send_g, recv_g, send_p, recv_p, send_f, recv_f, send_l, recv_l,
):
    tm, ti, h, c = position()
    z = tm // PLANE
    p = tm - z * PLANE
    size = sizes[0]
    blocks = z_count * PLANE
    mate = (tm, ti + 1 - 2 * c)
    cross = (tm, lax.rem(ti + 2, 4))
    before = (lax.rem(tm + blocks - 1, blocks), ti)
    after = (lax.rem(tm + 1, blocks), ti)

    def plane_peer(k, sign):
        q = lax.rem(p + PLANE + sign * (k % PLANE), PLANE)
        return z * PLANE + q, q, lax.rem(h + k // PLANE, 2)

    def plane_device(k):
        t, q, hh = plane_peer(k, 1)
        return (t, 2 * hh + c)

    def z_device(k):
        return (lax.rem(z + k, z_count) * PLANE + p, ti)

    greet([mate, before, after])
    greet([plane_device(k) for k in range(1, 2 * PLANE)])
    greet([z_device(k) for k in range(1, z_count)])

    lane = lax.broadcasted_iota(jnp.int32, (128, 128), 0)
    for group in range(4):
        picks = index[:, pl.ds(128 * group, 128)] - 128 * group
        hot = jnp.where(lane == picks, 1.0, 0.0).astype(BF)
        columns = pl.ds(128 * group, 128)
        g_perm[:, columns] = dot(g[:, columns], hot).astype(BF)

    def first_step(u):
        return 2.0 * u - product(product(u, kh[...], kl[...]), xh[...], xl[...])

    def rest(v):
        w = product(v, kh[...], kl[...])
        return 2.0 * v - first_step(product(w, xh[...], xl[...]))

    own_cols = pl.ds(al(128 * ti, 128), 128)
    g_cols = g_perm[:, own_cols].astype(F32).T.astype(BF)
    v = first_step(dot(g_cols, xh[...]) + dot(g_cols, xl[...]))
    y_high, y_low = split(rest(v))
    panel[...] = dot(y_high, g_perm[...]) + dot(y_low, g_perm[...])

    pl.semaphore_wait(pltpu.get_barrier_semaphore(), 3 + 2 * PLANE - 1 + z_count - 1)

    def part(q):
        return pl.ds(al(16 * q, 16), 16)

    sends_a = []
    for k in range(1, PLANE):
        t, q, _ = plane_peer(k, 1)
        made = remote(panel.at[part(q)], came_a.at[p], send_a.at[k], recv_a.at[k], (t, ti))
        made.start()
        sends_a.append(made)
    came_a[p] = panel[part(p), :]

    mine = pl.ds(al(ROWS * c, 64), ROWS)
    v = first_step(xh[mine, :].astype(F32) + xl[mine, :].astype(F32))
    wide[...] = rest(v)

    for made in sends_a:
        made.wait_recv()
    total = came_a[0]
    for q in range(1, PLANE):
        total = total + came_a[q]
    piece[...] = total

    def tile_of(first, j):
        return pl.ds(al(first + 8 * (j // 4), 8), 8), pl.ds(al(128 * (j % 4), 128), 128)

    order = sorted(range(1, z_count), key=lambda k: -min(k, z_count - k))
    sends_z = []
    for k in order:
        device = z_device(k)
        j = lax.rem(z + k, z_count) // 2
        made = remote(piece.at[tile_of(0, j)], came_z.at[z], send_z.at[k], recv_z.at[k], device)
        made.start()
        sends_z.append(made)
    jz = z // 2
    tile_rows, tile_cols = tile_of(0, jz)
    came_z[z] = piece[tile_rows, tile_cols]

    far = pl.ds(al(HALF + ROWS * c, 64), ROWS)
    my_start = pl.ds(al(128 * ti, 128), 128)
    cross_start = pl.ds(al(128 * lax.rem(ti + 2, 4), 128), 128)
    cross_pair = remote(pair_hbm, pair.at[far], send_l.at[0], recv_l.at[0], cross)
    cross_pair.start()
    cross_s = remote(start_hbm, start_f.at[my_start], send_l.at[1], recv_l.at[1], cross)
    cross_s.start()
    mate_pair = remote(pair_hbm, pair.at[mine], send_l.at[2], recv_l.at[2], mate)
    mate_pair.start()
    mate_s = remote(start_hbm, start_f.at[my_start], send_l.at[3], recv_l.at[3], mate)
    mate_s.start()
    local_pair = pltpu.make_async_copy(pair_hbm, pair.at[mine], local_sem.at[0])
    local_pair.start()
    local_s = pltpu.make_async_copy(start_hbm, start_f.at[my_start], local_sem.at[1])
    local_s.start()

    wide_high, wide_low = split(wide[...])
    yg[...] = dot(wide_high, g_perm[...]) + dot(wide_low, g_perm[...])

    for made in sends_z:
        made.wait_recv()
    total = came_z[0]
    for q in range(1, z_count):
        total = total + came_z[q]
    tile_rows, tile_cols = tile_of(16 * p, jz)
    own_piece = 16 * (PLANE * ti + p)
    at_rows, at_cols = tile_of(own_piece, jz)
    schur[at_rows, at_cols] = total + base[tile_rows, tile_cols]
    sends_g = []
    for k in sorted(range(2, z_count, 2), key=lambda k: -min(k, z_count - k)):
        here = schur.at[at_rows, at_cols]
        made = remote(here, here, send_g.at[k], recv_g.at[k], z_device(k))
        made.start()
        sends_g.append(made)

    cross_pair.wait_recv()
    pass_pair = remote(pair.at[far], pair.at[far], send_l.at[4], recv_l.at[4], mate)
    pass_pair.start()
    local_pair.wait()
    mate_pair.wait_recv()
    pass_pair.wait_recv()
    row = place_ids(h, 0, 0, 0, pair.shape)
    near[...] = jnp.where(row < size, pair[...].astype(F32), 0.0).astype(BF)
    which = lax.broadcasted_iota(jnp.int32, (128, 512), 0)
    wanted = jnp.where(which < 64, which + 64 * ti, which + (256 - 64) + 64 * ti)
    hot = jnp.where(lax.broadcasted_iota(jnp.int32, (128, 512), 1) == wanted, 1.0, 0.0).astype(BF)
    u = dot_nt(hot, near[...]).astype(BF)
    v = first_step(dot(u, xh[...]) + dot(u, xl[...]))
    y_high, y_low = split(rest(v))
    to_near = dot(y_high, near[...]) + dot(y_low, near[...])
    to_glob = dot(y_high, g_perm[...]) + dot(y_low, g_perm[...])
    nxt[:, pl.ds(0, 256)] = to_near[0:64, 0:256]
    nxt[:, pl.ds(256, 512)] = to_glob[0:64, :]
    next_copy = remote(nxt, nxt_came, send_l.at[5], recv_l.at[5], before)
    next_copy.start()
    off_out[...] = to_near[0:64, 256:512]
    diag_out[...] = to_near[64:128, 256:512]
    cross_out[...] = to_glob[64:128, :]
    cross_s.wait_recv()
    pass_s = remote(start_f.at[cross_start], start_f.at[cross_start], send_l.at[6], recv_l.at[6], mate)
    pass_s.start()

    for made in sends_g:
        made.wait_recv()

    def piece_of(hh, cc, q):
        return schur.at[pl.ds(al(16 * (PLANE * (2 * hh + cc) + q), 16), 16)]

    here = piece_of(h, c, p)
    sends_p = []
    for k in (9, 10, 11, 12, 13, 14, 15, 2, 3, 4, 5, 6, 1, 7, 8):
        made = remote(here, here, send_p.at[k], recv_p.at[k], plane_device(k))
        made.start()
        sends_p.append((k, made))
    passed = remote(here, here, send_f.at[0], recv_f.at[0], mate)
    passed.start()
    sends_f = [passed]

    local_s.wait()
    mate_s.wait_recv()
    pass_s.wait_recv()
    s_high[...], s_low[...] = split(start_f[...])
    back = product(yg[...], s_high[...], s_low[...])
    yg[...] = back
    next_copy.wait_recv()
    last = jnp.where(tm == blocks - 1, 0.0, 1.0).astype(F32)
    diag_out[...] += nxt_came[:, pl.ds(0, 256)] * last
    cross_out[...] += nxt_came[:, pl.ds(256, 512)] * last

    for k, made in sends_p:
        made.wait_recv()
        _, q, hh = plane_peer(k, -1)
        came = piece_of(hh, c, q)
        passed = remote(came, came, send_f.at[k], recv_f.at[k], mate)
        passed.start()
        sends_f.append(passed)
    for made in sends_f:
        made.wait_recv()

    t_high[...], t_low[...] = split(schur[...])
    schur_out[...] = schur[my_start, :]
    inner = product(yg[...], t_high[...], t_low[...])
    back_out[...] = 2.0 * yg[...] - product(inner, s_high[...], s_low[...])

    for made in sends_a + sends_z + sends_g + sends_f + [made for _, made in sends_p]:
        made.wait_send()
    for made in (cross_pair, cross_s, mate_pair, mate_s, pass_pair, next_copy, pass_s):
        made.wait_send()


VM = pl.BlockSpec(memory_space=pltpu.VMEM)
ANY = pl.BlockSpec(memory_space=pl.ANY)
SM = pl.BlockSpec(memory_space=pltpu.SMEM)
DMA = pltpu.SemaphoreType.DMA


def shards(operator, initial, block_sizes, link_index, link_pair, link_global, schur_base, schur_start):
    order = operator.shape[2]
    z_count = lax.axis_size("tm") // PLANE
    whole = jax.ShapeDtypeStruct((order, order), BF)
    xh, xl, kh, kl, g = pl.pallas_call(
        gather_kernel,
        out_shape=[whole] * 4 + [jax.ShapeDtypeStruct((order, 512), BF)],
        in_specs=[SM, ANY, ANY, ANY],
        out_specs=[VM] * 5,
        scratch_shapes=[
            pltpu.VMEM((HALF, order), F32),
            pltpu.VMEM((HALF, order), F32),
            pltpu.VMEM((HALF, HALF), F32),
            pltpu.VMEM((HALF, HALF), F32),
            pltpu.VMEM((order, 512), BF),
            DMA((5,)),
            DMA((19,)),
            DMA((19,)),
        ],
        compiler_params=pltpu.CompilerParams(collective_id=0, has_side_effects=True),
        name="gather_blocks",
    )(block_sizes, operator[0], initial[0], link_global[0])
    out = pl.pallas_call(
        functools.partial(reduce_kernel, z_count),
        out_shape=[
            jax.ShapeDtypeStruct((64, 256), F32),
            jax.ShapeDtypeStruct((64, 256), F32),
            jax.ShapeDtypeStruct((64, 512), F32),
            jax.ShapeDtypeStruct((128, 512), F32),
            jax.ShapeDtypeStruct((ROWS, 512), F32),
        ],
        in_specs=[SM] + [VM] * 7 + [ANY, ANY],
        out_specs=[VM] * 5,
        scratch_shapes=[
            pltpu.VMEM((order, 512), BF),
            pltpu.VMEM((128, 512), F32),
            pltpu.VMEM((PLANE, 16, 512), F32),
            pltpu.VMEM((16, 512), F32),
            pltpu.VMEM((z_count, 8, 128), F32),
            pltpu.VMEM((512, 512), F32),
            pltpu.VMEM((order, 512), BF),
            pltpu.VMEM((order, 512), BF),
            pltpu.VMEM((64, order), F32),
            pltpu.VMEM((64, order), F32),
            pltpu.VMEM((512, 512), F32),
            pltpu.VMEM((ROWS, 512), F32),
            pltpu.VMEM((ROWS, order), F32),
            pltpu.VMEM((512, 512), BF),
            pltpu.VMEM((512, 512), BF),
            pltpu.VMEM((512, 512), BF),
            pltpu.VMEM((512, 512), BF),
            DMA((2,)),
            DMA((PLANE,)), DMA((PLANE,)),
            DMA((z_count,)), DMA((z_count,)),
            DMA((z_count,)), DMA((z_count,)),
            DMA((2 * PLANE,)), DMA((2 * PLANE,)),
            DMA((2 * PLANE,)), DMA((2 * PLANE,)),
            DMA((7,)), DMA((7,)),
        ],
        compiler_params=pltpu.CompilerParams(collective_id=1, has_side_effects=True),
        name="chain_and_reduce",
    )(block_sizes, link_index, xh, xl, kh, kl, g, schur_base, link_pair[0], schur_start)
    diag, off, cross, schur, back = out
    return diag[None], off[None], cross[None], schur, back[None]


def solution(mesh):
    return jax.shard_map(
        shards,
        mesh=mesh,
        in_specs=(
            P("tm", "tile", None),
            P("tm", "tile", None),
            P("tm"),
            P("tm", None),
            P("tm", "tile", None),
            P("tm", "tile", None),
            P("tile", None),
            P("tile", None),
        ),
        out_specs=(
            P("tm", "tile", None),
            P("tm", "tile", None),
            P("tm", "tile", None),
            P("tile", None),
            P("tm", "tile", None),
        ),
        check_vma=False,
    )
```

```python
import functools

import jax
import jax.numpy as jnp
from jax import lax
from jax.experimental import pallas as pl
from jax.experimental.pallas import tpu as pltpu
from jax.sharding import PartitionSpec as P

MESH = pl.DeviceIdType.MESH
BF = jnp.bfloat16
F32 = jnp.float32
PLANE = 8
HALF = 384
ROWS = 192
GRANT = 32 << 20


def al(value, step):
    return pl.multiple_of(value, step)


def dot(left, right):
    return jnp.dot(left, right, preferred_element_type=F32)


def dot_nt(left, right):
    return lax.dot_general(left, right, (((1,), (1,)), ((), ())), preferred_element_type=F32)


def split(value):
    high = value.astype(BF)
    return high, (value - high.astype(F32)).astype(BF)


def product(value, high, low):
    value_high, value_low = split(value)
    return dot(value_high, high) + dot(value_high, low) + dot(value_low, high)


def position():
    tm = lax.axis_index("tm")
    ti = lax.axis_index("tile")
    h = ti // 2
    return tm, ti, h, ti - 2 * h


def remote(src, dst, send, recv, device):
    return pltpu.make_async_remote_copy(
        src_ref=src, dst_ref=dst, send_sem=send, recv_sem=recv, device_id=device, device_id_type=MESH
    )


def greet(devices):
    barrier = pltpu.get_barrier_semaphore()
    for device in devices:
        pl.semaphore_signal(barrier, inc=1, device_id=device, device_id_type=MESH)


def place_ids(h, first, axis, shape):
    ids = lax.broadcasted_iota(jnp.int32, shape, axis) + first
    return jnp.where(ids < HALF, ids + h * HALF, ids - h * HALF)


def block_kernel(
    z_count,
    sizes, k_hbm, x_hbm, g_hbm, pair_hbm, index_hbm, base_hbm, start_hbm,
    diag_out, off_out, cross_out, schur, w_out, s_high, s_low,
    xh, xl, kh, kl, rows_x, rows_k, diag_x, diag_k, rows_g, g_perm, index, base,
    panel, came_a, piece, came_z, pair, near, nxt, nxt_came, start_f, wide,
    local_sem, send_t, recv_t, send_a, recv_a, send_z, recv_z, send_g, recv_g, send_p, recv_p, send_f, recv_f, known,
):
    tm, ti, h, c = position()
    z = tm // PLANE
    p = tm - z * PLANE
    size = sizes[0]
    blocks = z_count * PLANE
    mate = (tm, ti + 1 - 2 * c)
    cross = (tm, lax.rem(ti + 2, 4))
    before = (lax.rem(tm + blocks - 1, blocks), ti)

    def plane_peer(k, sign):
        q = lax.rem(p + PLANE + sign * (k % PLANE), PLANE)
        return z * PLANE + q, q, lax.rem(h + k // PLANE, 2)

    def plane_device(k):
        t, q, hh = plane_peer(k, 1)
        return (t, 2 * hh + c)

    def z_device(k):
        return (lax.rem(z + k, z_count) * PLANE + p, ti)

    x_near = [plane_device(2), plane_device(PLANE - 2)]

    def z_near(by):
        return [z_device(by), z_device(z_count - by)]

    flip = p + 1 - 2 * lax.rem(p, 2)
    y_near = [(z * PLANE + flip, ti), (z * PLANE + flip, lax.rem(ti + 2, 4)), cross]
    greet(y_near + x_near + z_near(1) + [mate])

    def tell(round_, devices):
        for device in devices:
            pl.semaphore_signal(known.at[round_], inc=1, device_id=device, device_id_type=MESH)

    def hear(round_, count):
        pl.semaphore_wait(known.at[round_], count)

    own = al(h * HALF, 128)
    oth = al(HALF - h * HALF, 128)
    mine = pl.ds(al(ROWS * c, 64), ROWS)
    far = pl.ds(al(HALF + ROWS * c, 64), ROWS)
    my_start = pl.ds(al(128 * ti, 128), 128)
    cross_start = pl.ds(al(128 * lax.rem(ti + 2, 4), 128), 128)
    near_cols = pl.ds(al(256 * h, 256), 256)
    far_cols = pl.ds(al(256 - 256 * h, 256), 256)
    used = [0, 0]

    def copy(src, dst, device):
        at = used[0]
        used[0] += 1
        made = remote(src, dst, send_t.at[at], recv_t.at[at], device)
        made.start()
        sent.append(made)
        return made

    def local(src, dst):
        made = pltpu.make_async_copy(src, dst, local_sem.at[used[1]])
        used[1] += 1
        made.start()
        return made

    sent = []

    def pieces(ref):
        return [
            ref.at[pl.ds(al(256 * c, 128), 128), pl.ds(al(256 * c, 128), 128)],
            ref.at[pl.ds(al(256 * c, 128), 128), pl.ds(al(128 - 128 * c, 128), 128)],
            ref.at[pl.ds(al(128 + 64 * c, 64), 64), pl.ds(128, 256)],
        ]

    def sources(hbm):
        return [
            hbm.at[pl.ds(al(64 * c, 64), 128), pl.ds(al(own + 256 * c, 128), 128)],
            hbm.at[pl.ds(al(64 * c, 64), 128), pl.ds(al(own + 128 - 128 * c, 128), 128)],
            hbm.at[pl.ds(al(128 - 128 * c, 64), 64), pl.ds(al(own + 128, 128), 256)],
        ]

    def halves(hbm, rows):
        return [
            (hbm.at[:, pl.ds(own, HALF)], rows.at[mine, pl.ds(0, HALF)]),
            (hbm.at[:, pl.ds(oth, HALF)], rows.at[mine, pl.ds(HALF, HALF)]),
        ]

    local_g = local(g_hbm, rows_g.at[mine])
    local_x = [local(a, b) for a, b in halves(x_hbm, rows_x)]
    local_k = [local(a, b) for a, b in halves(k_hbm, rows_k)]
    local_index = local(index_hbm, index)
    local_pair = local(pair_hbm, pair.at[mine])
    local_base = local(base_hbm, base)
    local_s = local(start_hbm, start_f.at[my_start])

    pl.semaphore_wait(pltpu.get_barrier_semaphore(), 8)

    cross_g = copy(g_hbm.at[:, far_cols], rows_g.at[far, far_cols], cross)
    mate_g = copy(g_hbm, rows_g.at[mine], mate)
    cross_x = [copy(a, b, cross) for a, b in zip(sources(x_hbm), pieces(diag_x))]
    mate_x = [copy(a, b, mate) for a, b in halves(x_hbm, rows_x)]
    cross_k = [copy(a, b, cross) for a, b in zip(sources(k_hbm), pieces(diag_k))]
    mate_k = [copy(a, b, mate) for a, b in halves(k_hbm, rows_k)]
    cross_g_rest = copy(g_hbm.at[:, near_cols], rows_g.at[far, near_cols], cross)
    cross_pair = copy(pair_hbm, pair.at[far], cross)
    mate_pair = copy(pair_hbm, pair.at[mine], mate)
    tell(0, x_near)
    tell(1, z_near(1))

    def effective(block, first_row, first_col):
        row = place_ids(h, first_row, 0, block.shape)
        col = place_ids(h, first_col, 1, block.shape)
        unit = jnp.where(row == col, 1.0, 0.0).astype(F32)
        return jnp.where((row < size) & (col < size), block, unit)

    def store(high, low, row, col, value):
        n, m = value.shape
        value_high, value_low = split(value)
        high[pl.ds(row, n), pl.ds(col, m)] = value_high
        low[pl.ds(row, n), pl.ds(col, m)] = value_low

    def own_rows(rows, high, low):
        for i in range(3):
            at = 128 * i
            store(high, low, at, 0, effective(rows[pl.ds(at, 128), pl.ds(0, HALF)], at, 0))
            block = effective(rows[pl.ds(at, 128), pl.ds(HALF, HALF)], at, HALF)
            store(high, low, at, HALF, block)
            store(high, low, HALF, at, block.T)

    def far_rows(diag, high, low):
        for i in range(3):
            j = (i + 1) % 3
            at = HALF + 128 * i
            for col in (i, j):
                block = diag[pl.ds(128 * i, 128), pl.ds(128 * col, 128)]
                block = effective(block, at, HALF + 128 * col)
                store(high, low, at, HALF + 128 * col, block)
                if col == j:
                    store(high, low, HALF + 128 * j, at, block.T)

    def hand_on(came, refs):
        passed = []
        for made, ref in zip(came, refs):
            made.wait_recv()
            passed.append(copy(ref, ref, mate))
        return passed

    def arrive(copies):
        for made in copies:
            made.wait_recv()

    lane = lax.broadcasted_iota(jnp.int32, (128, 128), 0)

    def permute(first):
        columns = pl.ds(first, 128)
        hot = jnp.where(lane == index[:, columns] - first, 1.0, 0.0).astype(BF)
        picked = dot(rows_g[:, columns], hot)
        return jnp.where(place_ids(h, 0, 0, picked.shape) < size, picked, 0.0)

    def first_step(u):
        return 2.0 * u - product(product(u, kh[...], kl[...]), xh[...], xl[...])

    local_index.wait()
    local_g.wait()
    mate_g.wait_recv()
    pass_g = hand_on([cross_g], [rows_g.at[far, near_cols]])
    hear(0, 2)
    hear(1, 2)
    tell(2, x_near)
    tell(3, z_near(2))
    for made in local_x:
        made.wait()
    arrive(mate_x)
    own_rows(rows_x, xh, xl)
    arrive(pass_g)
    u = permute(al(128 * ti, 128)).T.astype(BF)
    pass_x = hand_on(cross_x, pieces(diag_x))
    hear(2, 2)
    hear(3, 2)
    tell(4, z_near(1))
    tell(5, z_near(4))
    for made in local_k:
        made.wait()
    arrive(mate_k)
    own_rows(rows_k, kh, kl)
    arrive(pass_x)
    far_rows(diag_x, xh, xl)
    v = dot(u, xh[...]) + dot(u, xl[...])
    pass_k = hand_on(cross_k, pieces(diag_k))
    arrive(pass_k)
    far_rows(diag_k, kh, kl)
    v = first_step(v)
    pass_g_rest = hand_on([cross_g_rest], [rows_g.at[far, far_cols]])
    w = product(product(v, kh[...], kl[...]), xh[...], xl[...])
    arrive(pass_g_rest)
    for group in range(4):
        g_perm[:, pl.ds(128 * group, 128)] = permute(128 * group).astype(BF)
    y_high, y_low = split(2.0 * v - first_step(w))
    pass_pair = hand_on([cross_pair], [pair.at[far]])
    panel[...] = dot(y_high, g_perm[...]) + dot(y_low, g_perm[...])

    hear(4, 2)
    hear(5, 2)

    def part(q):
        return pl.ds(al(16 * q, 16), 16)

    sends_a = []
    for k in range(1, PLANE):
        t, q, _ = plane_peer(k, 1)
        made = remote(panel.at[part(q)], came_a.at[p], send_a.at[k], recv_a.at[k], (t, ti))
        made.start()
        sends_a.append(made)
    came_a[p] = panel[part(p), :]

    local_pair.wait()
    mate_pair.wait_recv()
    arrive(pass_pair)
    row = place_ids(h, 0, 0, pair.shape)
    near[...] = jnp.where(row < size, pair[...].astype(F32), 0.0).astype(BF)
    which = lax.broadcasted_iota(jnp.int32, (128, 512), 0)
    wanted = jnp.where(which < 64, which + 64 * ti, which + (256 - 64) + 64 * ti)
    hot = jnp.where(lax.broadcasted_iota(jnp.int32, (128, 512), 1) == wanted, 1.0, 0.0).astype(BF)
    u = dot_nt(hot, near[...]).astype(BF)
    wide[pl.ds(0, 128), :] = first_step(dot(u, xh[...]) + dot(u, xl[...]))

    arrive(sends_a)
    total = came_a[0]
    for q in range(1, PLANE):
        total = total + came_a[q]
    piece[...] = total

    def tile_of(first, j):
        return pl.ds(al(first + 8 * (j // 4), 8), 8), pl.ds(al(128 * (j % 4), 128), 128)

    sends_z = []
    for k in sorted(range(1, z_count), key=lambda k: -min(k, z_count - k)):
        j = lax.rem(z + k, z_count) // 2
        made = remote(piece.at[tile_of(0, j)], came_z.at[z], send_z.at[k], recv_z.at[k], z_device(k))
        made.start()
        sends_z.append(made)
    jz = z // 2
    tile_rows, tile_cols = tile_of(0, jz)
    came_z[z] = piece[tile_rows, tile_cols]
    cross_s = copy(start_hbm, start_f.at[my_start], cross)
    mate_s = copy(start_hbm, start_f.at[my_start], mate)

    v = wide[pl.ds(0, 128), :]
    w = product(product(v, kh[...], kl[...]), xh[...], xl[...])
    y_high, y_low = split(2.0 * v - first_step(w))
    to_near = dot(y_high, near[...]) + dot(y_low, near[...])
    to_glob = dot(y_high, g_perm[...]) + dot(y_low, g_perm[...])
    nxt[:, pl.ds(0, 256)] = to_near[0:64, 0:256]
    nxt[:, pl.ds(256, 512)] = to_glob[0:64, :]
    next_copy = copy(nxt, nxt_came, before)
    off_out[...] = to_near[0:64, 256:512]
    diag_out[...] = to_near[64:128, 256:512]
    cross_out[...] = to_glob[64:128, :]
    local_base.wait()

    arrive(sends_z)
    total = came_z[0]
    for q in range(1, z_count):
        total = total + came_z[q]
    tile_rows, tile_cols = tile_of(16 * p, jz)
    at_rows, at_cols = tile_of(16 * (PLANE * ti + p), jz)
    schur[at_rows, at_cols] = total + base[tile_rows, tile_cols]
    sends_g = []
    for k in sorted(range(2, z_count, 2), key=lambda k: -min(k, z_count - k)):
        here = schur.at[at_rows, at_cols]
        made = remote(here, here, send_g.at[k], recv_g.at[k], z_device(k))
        made.start()
        sends_g.append(made)

    v = first_step(xh[mine, :].astype(F32) + xl[mine, :].astype(F32))
    pass_s = hand_on([cross_s], [start_f.at[cross_start]])
    w = product(product(v, kh[...], kl[...]), xh[...], xl[...])
    wide[...] = 2.0 * v - first_step(w)

    arrive(sends_g)

    def piece_of(hh, cc, q):
        return schur.at[pl.ds(al(16 * (PLANE * (2 * hh + cc) + q), 16), 16)]

    here = piece_of(h, c, p)
    sends_p = []
    for k in (9, 10, 11, 12, 13, 14, 15, 2, 3, 4, 5, 6, 1, 7, 8):
        made = remote(here, here, send_p.at[k], recv_p.at[k], plane_device(k))
        made.start()
        sends_p.append((k, made))
    passed = remote(here, here, send_f.at[0], recv_f.at[0], mate)
    passed.start()
    sends_f = [passed]

    wide_high, wide_low = split(wide[...])
    yg = dot(wide_high, g_perm[...]) + dot(wide_low, g_perm[...])
    local_s.wait()
    mate_s.wait_recv()
    arrive(pass_s)
    s_high[...], s_low[...] = split(start_f[...])
    w_out[...] = product(yg, s_high[...], s_low[...])

    for k, made in sends_p:
        made.wait_recv()
        _, q, hh = plane_peer(k, -1)
        came = piece_of(hh, c, q)
        passed = remote(came, came, send_f.at[k], recv_f.at[k], mate)
        passed.start()
        sends_f.append(passed)
    next_copy.wait_recv()
    last = jnp.where(tm == blocks - 1, 0.0, 1.0).astype(F32)
    diag_out[...] += nxt_came[:, pl.ds(0, 256)] * last
    cross_out[...] += nxt_came[:, pl.ds(256, 512)] * last
    arrive(sends_f)

    for made in sent + sends_a + sends_z + sends_g + sends_f + [made for _, made in sends_p]:
        made.wait_send()


def finish_kernel(
    diag, off, cross, schur, yg, s_high, s_low,
    diag_out, off_out, cross_out, schur_out, back_out,
    back, sem,
):
    mine = pl.ds(al(128 * lax.axis_index("tile"), 128), 128)
    pairs = ((diag, diag_out), (off, off_out), (cross, cross_out), (schur.at[mine], schur_out))
    copies = [pltpu.make_async_copy(a, b, sem.at[i]) for i, (a, b) in enumerate(pairs)]
    for made in copies:
        made.start()
    t_high, t_low = split(schur[...])
    for i in range(2):
        rows = pl.ds(96 * i, 96)
        inner = product(yg[rows, :], t_high, t_low)
        back[rows, :] = 2.0 * yg[rows, :] - product(inner, s_high[...], s_low[...])
        made = pltpu.make_async_copy(back.at[rows], back_out.at[rows], sem.at[4 + i])
        made.start()
        copies.append(made)
    for made in copies:
        made.wait()


VM = pl.BlockSpec(memory_space=pltpu.VMEM)
ANY = pl.BlockSpec(memory_space=pl.ANY)
HBM = pl.BlockSpec(memory_space=pltpu.HBM)
SM = pl.BlockSpec(memory_space=pltpu.SMEM)
DMA = pltpu.SemaphoreType.DMA


def shards(operator, initial, block_sizes, link_index, link_pair, link_global, schur_base, schur_start):
    order = operator.shape[2]
    z_count = lax.axis_size("tm") // PLANE
    out = pl.pallas_call(
        functools.partial(block_kernel, z_count),
        out_shape=[
            pltpu.VMEM((64, 256), F32),
            pltpu.VMEM((64, 256), F32),
            pltpu.VMEM((64, 512), F32),
            pltpu.VMEM((512, 512), F32),
            pltpu.VMEM((ROWS, 512), F32),
            pltpu.VMEM((512, 512), BF),
            pltpu.VMEM((512, 512), BF),
        ],
        in_specs=[SM] + [HBM] * 7,
        out_specs=[VM] * 7,
        scratch_shapes=[pltpu.VMEM((order, order), BF)] * 4
        + [pltpu.VMEM((HALF, order), F32)] * 2
        + [pltpu.VMEM((HALF, HALF), F32)] * 2
        + [
            pltpu.VMEM((order, 512), BF),
            pltpu.VMEM((order, 512), BF),
            pltpu.VMEM((1, 512), jnp.int32),
            pltpu.VMEM((128, 512), F32),
            pltpu.VMEM((128, 512), F32),
            pltpu.VMEM((PLANE, 16, 512), F32),
            pltpu.VMEM((16, 512), F32),
            pltpu.VMEM((z_count, 8, 128), F32),
            pltpu.VMEM((order, 512), BF),
            pltpu.VMEM((order, 512), BF),
            pltpu.VMEM((64, order), F32),
            pltpu.VMEM((64, order), F32),
            pltpu.VMEM((512, 512), F32),
            pltpu.VMEM((ROWS, order), F32),
            DMA((9,)),
            DMA((28,)), DMA((28,)),
            DMA((PLANE,)), DMA((PLANE,)),
            DMA((z_count,)), DMA((z_count,)),
            DMA((z_count,)), DMA((z_count,)),
            DMA((2 * PLANE,)), DMA((2 * PLANE,)),
            DMA((2 * PLANE,)), DMA((2 * PLANE,)),
            pltpu.SemaphoreType.REGULAR((6,)),
        ],
        compiler_params=pltpu.CompilerParams(collective_id=0, has_side_effects=True, vmem_limit_bytes=GRANT),
        name="block_step",
    )(
        block_sizes,
        *(
            pltpu.with_memory_space_constraint(array, pltpu.HBM)
            for array in (
                operator[0], initial[0], link_global[0], link_pair[0], link_index, schur_base, schur_start
            )
        ),
    )
    diag, off, cross, schur, back = pl.pallas_call(
        finish_kernel,
        out_shape=[
            jax.ShapeDtypeStruct((64, 256), F32),
            jax.ShapeDtypeStruct((64, 256), F32),
            jax.ShapeDtypeStruct((64, 512), F32),
            jax.ShapeDtypeStruct((128, 512), F32),
            jax.ShapeDtypeStruct((ROWS, 512), F32),
        ],
        in_specs=[VM] * 7,
        out_specs=[ANY] * 5,
        scratch_shapes=[pltpu.VMEM((ROWS, 512), F32), DMA((6,))],
        compiler_params=pltpu.CompilerParams(vmem_limit_bytes=GRANT),
        name="finish",
    )(*out)
    return diag[None], off[None], cross[None], schur, back[None]


def solution(mesh):
    return jax.shard_map(
        shards,
        mesh=mesh,
        in_specs=(
            P("tm", "tile", None),
            P("tm", "tile", None),
            P("tm"),
            P("tm", None),
            P("tm", "tile", None),
            P("tm", "tile", None),
            P("tile", None),
            P("tile", None),
        ),
        out_specs=(
            P("tm", "tile", None),
            P("tm", "tile", None),
            P("tm", "tile", None),
            P("tile", None),
            P("tm", "tile", None),
        ),
        check_vma=False,
    )
```

```python
import functools

import jax
import jax.numpy as jnp
from jax import lax
from jax.experimental import pallas as pl
from jax.experimental.pallas import tpu as pltpu
from jax.sharding import PartitionSpec as P

MESH = pl.DeviceIdType.MESH
BF = jnp.bfloat16
F32 = jnp.float32
PLANE = 8
HALF = 384
ROWS = 192
GRANT = 32 << 20


def al(value, step):
    return pl.multiple_of(value, step)


def dot(left, right):
    return jnp.dot(left, right, preferred_element_type=F32)


def dot_nt(left, right):
    return lax.dot_general(left, right, (((1,), (1,)), ((), ())), preferred_element_type=F32)


def split(value):
    high = value.astype(BF)
    return high, (value - high.astype(F32)).astype(BF)


def product(value, high, low):
    value_high, value_low = split(value)
    rows = value.shape[0]
    if rows > 128:
        return dot(value_high, high) + dot(value_high, low) + dot(value_low, high)
    both = dot(jnp.concatenate([value_high, value_low], axis=0), high)
    return both[:rows] + both[rows:] + dot(value_high, low)


def position():
    tm = lax.axis_index("tm")
    ti = lax.axis_index("tile")
    h = ti // 2
    return tm, ti, h, ti - 2 * h


def remote(src, dst, send, recv, device):
    return pltpu.make_async_remote_copy(
        src_ref=src, dst_ref=dst, send_sem=send, recv_sem=recv, device_id=device, device_id_type=MESH
    )


def drain(ref, sem):
    pltpu.make_async_copy(ref, ref, sem).wait()


def greet(devices):
    barrier = pltpu.get_barrier_semaphore()
    for device in devices:
        pl.semaphore_signal(barrier, inc=1, device_id=device, device_id_type=MESH)


def place_ids(h, first, axis, shape):
    ids = lax.broadcasted_iota(jnp.int32, shape, axis) + first
    return jnp.where(ids < HALF, ids + h * HALF, ids - h * HALF)


def block_kernel(
    z_count,
    sizes, k_hbm, x_hbm, g_hbm, pair_hbm, index_hbm, base_hbm, start_hbm,
    diag_out, off_out, cross_out, schur, w_out, inner_out, s_high, s_low,
    xh, xl, kh, kl, rows_x, rows_k, diag_x, diag_k, rows_g, g_perm, index, base,
    panel, came_a, piece, came_z, pair, near, nxt, nxt_came, start_f, wide,
    local_sem, send_sem, recv_t, recv_p, reduce_sem, known,
):
    tm, ti, h, c = position()
    z = tm // PLANE
    p = tm - z * PLANE
    blocks = z_count * PLANE
    mate = (tm, ti + 1 - 2 * c)
    cross = (tm, lax.rem(ti + 2, 4))
    before = (lax.rem(tm + blocks - 1, blocks), ti)

    def plane_peer(k, sign):
        q = lax.rem(p + PLANE + sign * (k % PLANE), PLANE)
        return z * PLANE + q, q, lax.rem(h + k // PLANE, 2)

    def plane_device(k):
        t, q, hh = plane_peer(k, 1)
        return (t, 2 * hh + c)

    def z_device(k):
        return (lax.rem(z + k, z_count) * PLANE + p, ti)

    x_near = [plane_device(2), plane_device(PLANE - 2)]

    def z_near(by):
        return [z_device(by), z_device(z_count - by)]

    flip = p + 1 - 2 * lax.rem(p, 2)
    y_near = [(z * PLANE + flip, ti), (z * PLANE + flip, lax.rem(ti + 2, 4)), cross]
    greet(y_near + x_near + z_near(1) + [mate])

    def tell(round_, devices):
        for device in devices:
            pl.semaphore_signal(known.at[round_], inc=1, device_id=device, device_id_type=MESH)

    def hear(round_, count):
        pl.semaphore_wait(known.at[round_], count)

    own = al(h * HALF, 128)
    oth = al(HALF - h * HALF, 128)
    mine = pl.ds(al(ROWS * c, 64), ROWS)
    far = pl.ds(al(HALF + ROWS * c, 64), ROWS)
    my_start = pl.ds(al(128 * ti, 128), 128)
    cross_start = pl.ds(al(128 * lax.rem(ti + 2, 4), 128), 128)
    near_cols = pl.ds(al(256 * h, 256), 256)
    far_cols = pl.ds(al(256 - 256 * h, 256), 256)
    used = [0, 0]

    def slot(kind):
        used[kind] += 1
        return used[kind] - 1

    def copy(src, dst, device, group, at=None):
        made = remote(src, dst, send_sem.at[group], recv_t.at[slot(0) if at is None else at], device)
        made.start()
        return made

    def local(src, dst, at=None):
        made = pltpu.make_async_copy(src, dst, local_sem.at[slot(1) if at is None else at])
        made.start()
        return made

    def pieces(ref):
        return [
            ref.at[pl.ds(al(256 * c, 128), 128), pl.ds(al(256 * c, 128), 128)],
            ref.at[pl.ds(al(256 * c, 128), 128), pl.ds(al(128 - 128 * c, 128), 128)],
            ref.at[pl.ds(al(128 + 64 * c, 64), 64), pl.ds(128, 256)],
        ]

    def sources(hbm):
        return [
            hbm.at[pl.ds(al(64 * c, 64), 128), pl.ds(al(own + 256 * c, 128), 128)],
            hbm.at[pl.ds(al(64 * c, 64), 128), pl.ds(al(own + 128 - 128 * c, 128), 128)],
            hbm.at[pl.ds(al(128 - 128 * c, 64), 64), pl.ds(al(own + 128, 128), 256)],
        ]

    def halves(hbm, rows):
        return [
            (hbm.at[:, pl.ds(own, HALF)], rows.at[mine, pl.ds(0, HALF)]),
            (hbm.at[:, pl.ds(oth, HALF)], rows.at[mine, pl.ds(HALF, HALF)]),
        ]

    local_g = local(g_hbm, rows_g.at[mine])
    local_x, local_k = slot(1), slot(1)
    for src, dst in halves(x_hbm, rows_x):
        local(src, dst, local_x)
    for src, dst in halves(k_hbm, rows_k):
        local(src, dst, local_k)
    local_index = local(index_hbm, index)
    local_pair = local(pair_hbm, pair.at[mine])
    local_base = local(base_hbm, base)
    local_s = local(start_hbm, start_f.at[my_start])

    pl.semaphore_wait(pltpu.get_barrier_semaphore(), 8)

    cross_g = copy(g_hbm.at[:, far_cols], rows_g.at[far, far_cols], cross, 0)
    mate_g = copy(g_hbm, rows_g.at[mine], mate, 0)
    cross_x = [copy(a, b, cross, 1) for a, b in zip(sources(x_hbm), pieces(diag_x))]
    mate_x, mate_k, pass_x, pass_k = slot(0), slot(0), slot(0), slot(0)
    for src, dst in halves(x_hbm, rows_x):
        copy(src, dst, mate, 1, mate_x)
    cross_k = [copy(a, b, cross, 2) for a, b in zip(sources(k_hbm), pieces(diag_k))]
    for src, dst in halves(k_hbm, rows_k):
        copy(src, dst, mate, 2, mate_k)
    cross_g_rest = copy(g_hbm.at[:, near_cols], rows_g.at[far, near_cols], cross, 0)
    cross_pair = copy(pair_hbm, pair.at[far], cross, 0)
    mate_pair = copy(pair_hbm, pair.at[mine], mate, 0)
    tell(0, x_near)
    tell(1, z_near(1))

    def effective(block, first_row, first_col):
        row = place_ids(h, first_row, 0, block.shape)
        col = place_ids(h, first_col, 1, block.shape)
        unit = jnp.where(row == col, 1.0, 0.0).astype(F32)
        return jnp.where((row < size) & (col < size), block, unit)

    def store(high, low, row, col, value):
        n, m = value.shape
        value_high, value_low = split(value)
        high[pl.ds(row, n), pl.ds(col, m)] = value_high
        low[pl.ds(row, n), pl.ds(col, m)] = value_low

    def own_rows(rows, high, low):
        for i in range(3):
            at = 128 * i
            store(high, low, at, 0, effective(rows[pl.ds(at, 128), pl.ds(0, HALF)], at, 0))
            block = effective(rows[pl.ds(at, 128), pl.ds(HALF, HALF)], at, HALF)
            store(high, low, at, HALF, block)
            store(high, low, HALF, at, block.T)

    def far_rows(diag, high, low):
        for i in range(3):
            j = (i + 1) % 3
            at = HALF + 128 * i
            for col in (i, j):
                block = diag[pl.ds(128 * i, 128), pl.ds(128 * col, 128)]
                block = effective(block, at, HALF + 128 * col)
                store(high, low, at, HALF + 128 * col, block)
                if col == j:
                    store(high, low, HALF + 128 * j, at, block.T)

    def hand_on(came, ref, group=3, at=None):
        came.wait_recv()
        return copy(ref, ref, mate, group, at)

    lane = lax.broadcasted_iota(jnp.int32, (128, 128), 0)

    def permute(first):
        columns = pl.ds(first, 128)
        hot = jnp.where(lane == index[:, columns] - first, 1.0, 0.0).astype(BF)
        picked = dot(rows_g[:, columns], hot)
        return jnp.where(place_ids(h, 0, 0, picked.shape) < size, picked, 0.0)

    def first_step(u):
        return 2.0 * u - product(product(u, kh[...], kl[...]), xh[...], xl[...])

    size = sizes[0]
    local_index.wait()
    local_g.wait()
    mate_g.wait_recv()
    pass_g = hand_on(cross_g, rows_g.at[far, near_cols])
    hear(0, 2)
    hear(1, 2)
    tell(2, x_near)
    tell(3, z_near(2))
    drain(rows_x.at[mine], local_sem.at[local_x])
    drain(rows_x.at[mine], recv_t.at[mate_x])
    own_rows(rows_x, xh, xl)
    pass_g.wait_recv()
    u = permute(al(128 * ti, 128)).T.astype(BF)
    for made, ref in zip(cross_x, pieces(diag_x)):
        hand_on(made, ref, 3, pass_x)
    hear(2, 2)
    hear(3, 2)
    tell(4, z_near(1))
    tell(5, z_near(4))
    drain(rows_k.at[mine], local_sem.at[local_k])
    drain(rows_k.at[mine], recv_t.at[mate_k])
    own_rows(rows_k, kh, kl)
    drain(rows_x.at[pl.ds(0, 64)], recv_t.at[pass_x])
    far_rows(diag_x, xh, xl)
    v = dot(u, xh[...]) + dot(u, xl[...])
    for made, ref in zip(cross_k, pieces(diag_k)):
        hand_on(made, ref, 3, pass_k)
    drain(rows_x.at[pl.ds(0, 64)], recv_t.at[pass_k])
    far_rows(diag_k, kh, kl)
    v = first_step(v)
    pass_g_rest = hand_on(cross_g_rest, rows_g.at[far, far_cols])
    w = product(product(v, kh[...], kl[...]), xh[...], xl[...])
    pass_g_rest.wait_recv()
    for group in range(4):
        g_perm[:, pl.ds(128 * group, 128)] = permute(128 * group).astype(BF)
    y_high, y_low = split(2.0 * v - first_step(w))
    pass_pair = hand_on(cross_pair, pair.at[far])
    panel[...] = dot(y_high, g_perm[...]) + dot(y_low, g_perm[...])

    hear(4, 2)
    hear(5, 2)

    def part(q):
        return pl.ds(al(16 * q, 16), 16)

    for k in range(1, PLANE):
        t, q, _ = plane_peer(k, 1)
        remote(panel.at[part(q)], came_a.at[p], reduce_sem.at[0], reduce_sem.at[1], (t, ti)).start()
    came_a[p] = panel[part(p), :]

    local_pair.wait()
    mate_pair.wait_recv()
    pass_pair.wait_recv()
    row = place_ids(h, 0, 0, pair.shape)
    near[...] = jnp.where(row < size, pair[...].astype(F32), 0.0).astype(BF)
    which = lax.broadcasted_iota(jnp.int32, (128, 512), 0)
    wanted = jnp.where(which < 64, which + 64 * ti, which + (256 - 64) + 64 * ti)
    hot = jnp.where(lax.broadcasted_iota(jnp.int32, (128, 512), 1) == wanted, 1.0, 0.0).astype(BF)
    u = dot_nt(hot, near[...]).astype(BF)
    wide[pl.ds(0, 128), :] = first_step(dot(u, xh[...]) + dot(u, xl[...]))

    others_a = came_a.at[pl.ds(0, PLANE - 1)]
    drain(others_a, reduce_sem.at[1])
    total = came_a[0]
    for q in range(1, PLANE):
        total = total + came_a[q]
    piece[...] = total

    def tile_of(first, j):
        return pl.ds(al(first + 8 * (j // 4), 8), 8), pl.ds(al(128 * (j % 4), 128), 128)

    for k in sorted(range(1, z_count), key=lambda k: -min(k, z_count - k)):
        j = lax.rem(z + k, z_count) // 2
        remote(piece.at[tile_of(0, j)], came_z.at[z], reduce_sem.at[2], reduce_sem.at[3], z_device(k)).start()
    jz = z // 2
    tile_rows, tile_cols = tile_of(0, jz)
    came_z[z] = piece[tile_rows, tile_cols]
    cross_s = copy(start_hbm, start_f.at[my_start], cross, 4)
    mate_s = copy(start_hbm, start_f.at[my_start], mate, 4)

    v = wide[pl.ds(0, 128), :]
    w = product(product(v, kh[...], kl[...]), xh[...], xl[...])
    y_high, y_low = split(2.0 * v - first_step(w))
    to_near = dot(y_high, near[...]) + dot(y_low, near[...])
    to_glob = dot(y_high, g_perm[...]) + dot(y_low, g_perm[...])
    nxt[:, pl.ds(0, 256)] = to_near[0:64, 0:256]
    nxt[:, pl.ds(256, 512)] = to_glob[0:64, :]
    next_copy = copy(nxt, nxt_came, before, 5)
    off_out[...] = to_near[0:64, 256:512]
    diag_out[...] = to_near[64:128, 256:512]
    cross_out[...] = to_glob[64:128, :]
    local_base.wait()
    wide[...] = first_step(xh[mine, :].astype(F32) + xl[mine, :].astype(F32))

    others_z = came_z.at[pl.ds(0, z_count - 1)]
    drain(others_z, reduce_sem.at[3])
    total = came_z[0]
    for q in range(1, z_count):
        total = total + came_z[q]
    tile_rows, tile_cols = tile_of(16 * p, jz)
    at_rows, at_cols = tile_of(16 * (PLANE * ti + p), jz)
    schur[at_rows, at_cols] = total + base[tile_rows, tile_cols]
    for k in sorted(range(2, z_count, 2), key=lambda k: -min(k, z_count - k)):
        here = schur.at[at_rows, at_cols]
        remote(here, here, reduce_sem.at[4], reduce_sem.at[5], z_device(k)).start()

    v = wide[...]
    w = product(product(v, kh[...], kl[...]), xh[...], xl[...])
    wide[...] = 2.0 * v - first_step(w)

    others_g = came_z.at[pl.ds(0, z_count // 2 - 1)]
    drain(others_g, reduce_sem.at[5])

    def piece_of(hh, cc, q):
        return schur.at[pl.ds(al(16 * (PLANE * (2 * hh + cc) + q), 16), 16)]

    here = piece_of(h, c, p)
    sends_p = []
    for k in (9, 10, 11, 12, 13, 14, 15, 2, 3, 4, 5, 6, 1, 7, 8):
        made = remote(here, here, reduce_sem.at[6], recv_p.at[k], plane_device(k))
        made.start()
        sends_p.append((k, made))
    remote(here, here, reduce_sem.at[7], reduce_sem.at[8], mate).start()
    pass_s = hand_on(cross_s, start_f.at[cross_start], 4)

    wide_high, wide_low = split(wide[...])
    yg = dot(wide_high, g_perm[...]) + dot(wide_low, g_perm[...])
    local_s.wait()
    mate_s.wait_recv()
    pass_s.wait_recv()
    s_high[...], s_low[...] = split(start_f[...])
    w_out[...] = product(yg, s_high[...], s_low[...])

    for k, made in sends_p:
        made.wait_recv()
        _, q, hh = plane_peer(k, -1)
        came = piece_of(hh, c, q)
        remote(came, came, reduce_sem.at[7], reduce_sem.at[8], mate).start()
    inner_out[...] = half_inner(c, w_out, schur)
    next_copy.wait_recv()
    last = jnp.where(tm == blocks - 1, 0.0, 1.0).astype(F32)
    diag_out[...] += nxt_came[:, pl.ds(0, 256)] * last
    cross_out[...] += nxt_came[:, pl.ds(256, 512)] * last
    others_p = schur.at[pl.ds(0, 16 * (2 * PLANE - 1))]
    everything = schur.at[pl.ds(0, 32 * PLANE)]
    drain(everything, reduce_sem.at[8])

    for group in range(5):
        drain(rows_x.at[pl.ds(0, 256)], send_sem.at[group])
    next_copy.wait_send()
    drain(others_a, reduce_sem.at[0])
    drain(others_z, reduce_sem.at[2])
    drain(others_g, reduce_sem.at[4])
    drain(others_p, reduce_sem.at[6])
    drain(everything, reduce_sem.at[7])


def half_inner(which, w, schur):
    first = pl.ds(al(128 * which, 128), 128)
    second = pl.ds(al(256 + 128 * which, 128), 128)
    t_high, t_low = split(jnp.concatenate([schur[first, :], schur[second, :]], axis=0))
    return product(jnp.concatenate([w[:, first], w[:, second]], axis=1), t_high, t_low)


def finish_kernel(
    diag, off, cross, schur, w, inner, s_high, s_low,
    diag_out, off_out, cross_out, schur_out, back_out,
    back, sem,
):
    mine = pl.ds(al(128 * lax.axis_index("tile"), 128), 128)
    pairs = ((diag, diag_out), (off, off_out), (cross, cross_out), (schur.at[mine], schur_out))
    copies = [pltpu.make_async_copy(a, b, sem.at[i]) for i, (a, b) in enumerate(pairs)]
    for made in copies:
        made.start()
    ti = lax.axis_index("tile")
    whole = inner[...] + half_inner(1 - lax.rem(ti, 2), w, schur)
    for i in range(2):
        rows = pl.ds(96 * i, 96)
        back[rows, :] = 2.0 * w[rows, :] - product(whole[96 * i : 96 * (i + 1)], s_high[...], s_low[...])
        made = pltpu.make_async_copy(back.at[rows], back_out.at[rows], sem.at[4 + i])
        made.start()
        copies.append(made)
    for made in copies:
        made.wait()


VM = pl.BlockSpec(memory_space=pltpu.VMEM)
SM = pl.BlockSpec(memory_space=pltpu.SMEM)
ANY = pl.BlockSpec(memory_space=pl.ANY)
HBM = pl.BlockSpec(memory_space=pltpu.HBM)
DMA = pltpu.SemaphoreType.DMA


def shards(operator, initial, block_sizes, link_index, link_pair, link_global, schur_base, schur_start):
    order = operator.shape[2]
    z_count = lax.axis_size("tm") // PLANE
    out = pl.pallas_call(
        functools.partial(block_kernel, z_count),
        out_shape=[
            pltpu.VMEM((64, 256), F32),
            pltpu.VMEM((64, 256), F32),
            pltpu.VMEM((64, 512), F32),
            pltpu.VMEM((512, 512), F32),
            pltpu.VMEM((ROWS, 512), F32),
            pltpu.VMEM((ROWS, 512), F32),
            pltpu.VMEM((512, 512), BF),
            pltpu.VMEM((512, 512), BF),
        ],
        in_specs=[SM] + [HBM] * 7,
        out_specs=[VM] * 8,
        scratch_shapes=[pltpu.VMEM((order, order), BF)] * 4
        + [pltpu.VMEM((HALF, order), F32)] * 2
        + [pltpu.VMEM((HALF, HALF), F32)] * 2
        + [
            pltpu.VMEM((order, 512), BF),
            pltpu.VMEM((order, 512), BF),
            pltpu.VMEM((1, 512), jnp.int32),
            pltpu.VMEM((128, 512), F32),
            pltpu.VMEM((128, 512), F32),
            pltpu.VMEM((PLANE, 16, 512), F32),
            pltpu.VMEM((16, 512), F32),
            pltpu.VMEM((z_count, 8, 128), F32),
            pltpu.VMEM((order, 512), BF),
            pltpu.VMEM((order, 512), BF),
            pltpu.VMEM((64, order), F32),
            pltpu.VMEM((64, order), F32),
            pltpu.VMEM((512, 512), F32),
            pltpu.VMEM((ROWS, order), F32),
            DMA((7,)),
            DMA((6,)),
            DMA((22,)),
            DMA((2 * PLANE,)),
            DMA((9,)),
            pltpu.SemaphoreType.REGULAR((6,)),
        ],
        compiler_params=pltpu.CompilerParams(collective_id=0, has_side_effects=True, vmem_limit_bytes=GRANT),
        name="block_step",
    )(
        block_sizes,
        *(
            pltpu.with_memory_space_constraint(array, pltpu.HBM)
            for array in (
                operator[0], initial[0], link_global[0], link_pair[0], link_index, schur_base, schur_start
            )
        ),
    )
    diag, off, cross, schur, back = pl.pallas_call(
        finish_kernel,
        out_shape=[
            jax.ShapeDtypeStruct((64, 256), F32),
            jax.ShapeDtypeStruct((64, 256), F32),
            jax.ShapeDtypeStruct((64, 512), F32),
            jax.ShapeDtypeStruct((128, 512), F32),
            jax.ShapeDtypeStruct((ROWS, 512), F32),
        ],
        in_specs=[VM] * 8,
        out_specs=[ANY] * 5,
        scratch_shapes=[pltpu.VMEM((ROWS, 512), F32), DMA((6,))],
        compiler_params=pltpu.CompilerParams(vmem_limit_bytes=GRANT),
        name="finish",
    )(*out)
    return diag[None], off[None], cross[None], schur, back[None]


def solution(mesh):
    return jax.shard_map(
        shards,
        mesh=mesh,
        in_specs=(
            P("tm", "tile", None),
            P("tm", "tile", None),
            P("tm"),
            P("tm", None),
            P("tm", "tile", None),
            P("tm", "tile", None),
            P("tile", None),
            P("tile", None),
        ),
        out_specs=(
            P("tm", "tile", None),
            P("tm", "tile", None),
            P("tm", "tile", None),
            P("tile", None),
            P("tm", "tile", None),
        ),
        check_vma=False,
    )
```

```python
import functools

import jax
import jax.numpy as jnp
from jax import lax
from jax.experimental import pallas as pl
from jax.experimental.pallas import tpu as pltpu
from jax.sharding import PartitionSpec as P

MESH = pl.DeviceIdType.MESH
BF = jnp.bfloat16
F32 = jnp.float32
PLANE = 8
HALF = 384
ROWS = 192
GRANT = 32 << 20
COMES = (0, 1, 2, 7, 6, 3, 4, 5)
EARLY = 5


def al(value, step):
    return pl.multiple_of(value, step)


def dot(left, right):
    return jnp.dot(left, right, preferred_element_type=F32)


def dot_nt(left, right):
    return lax.dot_general(left, right, (((1,), (1,)), ((), ())), preferred_element_type=F32)


def split(value):
    high = value.astype(BF)
    return high, (value - high.astype(F32)).astype(BF)


def product(value, high, low):
    value_high, value_low = split(value)
    rows = value.shape[0]
    if rows > 128:
        return dot(value_high, high) + dot(value_high, low) + dot(value_low, high)
    both = dot(jnp.concatenate([value_high, value_low], axis=0), high)
    return both[:rows] + both[rows:] + dot(value_high, low)


def position():
    tm = lax.axis_index("tm")
    ti = lax.axis_index("tile")
    h = ti // 2
    return tm, ti, h, ti - 2 * h


def remote(src, dst, send, recv, device):
    return pltpu.make_async_remote_copy(
        src_ref=src, dst_ref=dst, send_sem=send, recv_sem=recv, device_id=device, device_id_type=MESH
    )


def drain(ref, sem):
    pltpu.make_async_copy(ref, ref, sem).wait()


def greet(devices):
    barrier = pltpu.get_barrier_semaphore()
    for device in devices:
        pl.semaphore_signal(barrier, inc=1, device_id=device, device_id_type=MESH)


def place_ids(h, first, axis, shape):
    ids = lax.broadcasted_iota(jnp.int32, shape, axis) + first
    return jnp.where(ids < HALF, ids + h * HALF, ids - h * HALF)


def block_kernel(
    z_count,
    sizes, k_hbm, x_hbm, g_hbm, pair_hbm, index_hbm, base_hbm, start_hbm,
    diag_out, off_out, cross_out, schur, w_out, inner_out, s_high, s_low,
    xh, xl, kh, kl, rows_x, rows_k, diag_x, diag_k, rows_g, g_perm, index, base,
    panel, came_a, piece, came_z, tiles, pair, near, nxt, nxt_came, start_f, wide,
    local_sem, send_sem, recv_t, recv_p, reduce_sem, known,
):
    tm, ti, h, c = position()
    z = tm // PLANE
    p = tm - z * PLANE
    blocks = z_count * PLANE
    mate = (tm, ti + 1 - 2 * c)
    cross = (tm, lax.rem(ti + 2, 4))
    before = (lax.rem(tm + blocks - 1, blocks), ti)

    def plane_peer(k, sign):
        q = lax.rem(p + PLANE + sign * (k % PLANE), PLANE)
        return z * PLANE + q, q, lax.rem(h + k // PLANE, 2)

    def plane_device(k):
        t, q, hh = plane_peer(k, 1)
        return (t, 2 * hh + c)

    def z_device(k):
        return (lax.rem(z + k, z_count) * PLANE + p, ti)

    x_near = [plane_device(2), plane_device(PLANE - 2)]

    def z_near(by):
        return [z_device(by), z_device(z_count - by)]

    flip = p + 1 - 2 * lax.rem(p, 2)
    y_near = [(z * PLANE + flip, ti), (z * PLANE + flip, lax.rem(ti + 2, 4)), cross]
    greet(y_near + x_near + z_near(1) + [mate])

    def tell(round_, devices):
        for device in devices:
            pl.semaphore_signal(known.at[round_], inc=1, device_id=device, device_id_type=MESH)

    def hear(round_, count):
        pl.semaphore_wait(known.at[round_], count)

    own = al(h * HALF, 128)
    oth = al(HALF - h * HALF, 128)
    mine = pl.ds(al(ROWS * c, 64), ROWS)
    far = pl.ds(al(HALF + ROWS * c, 64), ROWS)
    my_start = pl.ds(al(128 * ti, 128), 128)
    cross_start = pl.ds(al(128 * lax.rem(ti + 2, 4), 128), 128)
    near_cols = pl.ds(al(256 * h, 256), 256)
    far_cols = pl.ds(al(256 - 256 * h, 256), 256)
    used = [0, 0]

    def slot(kind):
        used[kind] += 1
        return used[kind] - 1

    def copy(src, dst, device, group, at=None):
        made = remote(src, dst, send_sem.at[group], recv_t.at[slot(0) if at is None else at], device)
        made.start()
        return made

    def local(src, dst, at=None):
        made = pltpu.make_async_copy(src, dst, local_sem.at[slot(1) if at is None else at])
        made.start()
        return made

    def pieces(ref):
        return [
            ref.at[pl.ds(al(256 * c, 128), 128), pl.ds(al(256 * c, 128), 128)],
            ref.at[pl.ds(al(256 * c, 128), 128), pl.ds(al(128 - 128 * c, 128), 128)],
            ref.at[pl.ds(al(128 + 64 * c, 64), 64), pl.ds(128, 256)],
        ]

    def sources(hbm):
        return [
            hbm.at[pl.ds(al(64 * c, 64), 128), pl.ds(al(own + 256 * c, 128), 128)],
            hbm.at[pl.ds(al(64 * c, 64), 128), pl.ds(al(own + 128 - 128 * c, 128), 128)],
            hbm.at[pl.ds(al(128 - 128 * c, 64), 64), pl.ds(al(own + 128, 128), 256)],
        ]

    def halves(hbm, rows):
        return [
            (hbm.at[:, pl.ds(own, HALF)], rows.at[mine, pl.ds(0, HALF)]),
            (hbm.at[:, pl.ds(oth, HALF)], rows.at[mine, pl.ds(HALF, HALF)]),
        ]

    local_g = local(g_hbm, rows_g.at[mine])
    local_x, local_k = slot(1), slot(1)
    for src, dst in halves(x_hbm, rows_x):
        local(src, dst, local_x)
    for src, dst in halves(k_hbm, rows_k):
        local(src, dst, local_k)
    local_index = local(index_hbm, index)
    local_pair = local(pair_hbm, pair.at[mine])
    local_base = local(base_hbm, base)
    local_s = local(start_hbm, start_f.at[my_start])

    pl.semaphore_wait(pltpu.get_barrier_semaphore(), 8)

    cross_g = copy(g_hbm.at[:, far_cols], rows_g.at[far, far_cols], cross, 0)
    mate_g = copy(g_hbm, rows_g.at[mine], mate, 0)
    cross_x = [copy(a, b, cross, 1) for a, b in zip(sources(x_hbm), pieces(diag_x))]
    mate_x, mate_k, pass_x, pass_k = slot(0), slot(0), slot(0), slot(0)
    for src, dst in halves(x_hbm, rows_x):
        copy(src, dst, mate, 1, mate_x)
    cross_k = [copy(a, b, cross, 2) for a, b in zip(sources(k_hbm), pieces(diag_k))]
    for src, dst in halves(k_hbm, rows_k):
        copy(src, dst, mate, 2, mate_k)
    cross_g_rest = copy(g_hbm.at[:, near_cols], rows_g.at[far, near_cols], cross, 0)
    cross_pair = copy(pair_hbm, pair.at[far], cross, 0)
    mate_pair = copy(pair_hbm, pair.at[mine], mate, 0)
    tell(0, x_near)
    tell(1, z_near(1))

    def effective(block, first_row, first_col):
        row = place_ids(h, first_row, 0, block.shape)
        col = place_ids(h, first_col, 1, block.shape)
        unit = jnp.where(row == col, 1.0, 0.0).astype(F32)
        return jnp.where((row < size) & (col < size), block, unit)

    def store(high, low, row, col, value):
        n, m = value.shape
        value_high, value_low = split(value)
        high[pl.ds(row, n), pl.ds(col, m)] = value_high
        low[pl.ds(row, n), pl.ds(col, m)] = value_low

    def own_rows(rows, high, low):
        for i in range(3):
            at = 128 * i
            store(high, low, at, 0, effective(rows[pl.ds(at, 128), pl.ds(0, HALF)], at, 0))
            block = effective(rows[pl.ds(at, 128), pl.ds(HALF, HALF)], at, HALF)
            store(high, low, at, HALF, block)
            store(high, low, HALF, at, block.T)

    def far_rows(diag, high, low):
        for i in range(3):
            j = (i + 1) % 3
            at = HALF + 128 * i
            for col in (i, j):
                block = diag[pl.ds(128 * i, 128), pl.ds(128 * col, 128)]
                block = effective(block, at, HALF + 128 * col)
                store(high, low, at, HALF + 128 * col, block)
                if col == j:
                    store(high, low, HALF + 128 * j, at, block.T)

    def hand_on(came, ref, group=3, at=None):
        came.wait_recv()
        return copy(ref, ref, mate, group, at)

    lane = lax.broadcasted_iota(jnp.int32, (128, 128), 0)

    def permute(first):
        columns = pl.ds(first, 128)
        hot = jnp.where(lane == index[:, columns] - first, 1.0, 0.0).astype(BF)
        picked = dot(rows_g[:, columns], hot)
        return jnp.where(place_ids(h, 0, 0, picked.shape) < size, picked, 0.0)

    def first_step(u):
        return 2.0 * u - product(product(u, kh[...], kl[...]), xh[...], xl[...])

    size = sizes[0]
    local_index.wait()
    local_g.wait()
    mate_g.wait_recv()
    pass_g = hand_on(cross_g, rows_g.at[far, near_cols])
    hear(0, 2)
    hear(1, 2)
    tell(2, x_near)
    tell(3, z_near(2))
    drain(rows_x.at[mine], local_sem.at[local_x])
    drain(rows_x.at[mine], recv_t.at[mate_x])
    own_rows(rows_x, xh, xl)
    pass_g.wait_recv()
    u = permute(al(128 * ti, 128)).T.astype(BF)
    for made, ref in zip(cross_x, pieces(diag_x)):
        hand_on(made, ref, 3, pass_x)
    hear(2, 2)
    hear(3, 2)
    tell(4, z_near(1))
    tell(5, z_near(4))
    drain(rows_k.at[mine], local_sem.at[local_k])
    drain(rows_k.at[mine], recv_t.at[mate_k])
    own_rows(rows_k, kh, kl)
    drain(rows_x.at[pl.ds(0, 64)], recv_t.at[pass_x])
    far_rows(diag_x, xh, xl)
    v = dot(u, xh[...]) + dot(u, xl[...])
    w_own = product(v, kh[:, pl.ds(0, HALF)], kl[:, pl.ds(0, HALF)])
    first, second = pl.ds(0, HALF), pl.ds(HALF, HALF)
    w_far = product(v[:, :HALF], kh[first, second], kl[first, second])
    for made, ref in zip(cross_k, pieces(diag_k)):
        hand_on(made, ref, 3, pass_k)
    drain(rows_x.at[pl.ds(0, 64)], recv_t.at[pass_k])
    far_rows(diag_k, kh, kl)
    w_far = w_far + product(v[:, HALF:], kh[second, second], kl[second, second])
    v = 2.0 * v - product(jnp.concatenate([w_own, w_far], axis=1), xh[...], xl[...])
    pass_g_rest = hand_on(cross_g_rest, rows_g.at[far, far_cols])
    w = product(product(v, kh[...], kl[...]), xh[...], xl[...])
    pass_g_rest.wait_recv()
    for group in range(4):
        g_perm[:, pl.ds(128 * group, 128)] = permute(128 * group).astype(BF)
    y_high, y_low = split(2.0 * v - first_step(w))
    pass_pair = hand_on(cross_pair, pair.at[far])
    panel[...] = dot(y_high, g_perm[...]) + dot(y_low, g_perm[...])

    hear(4, 2)
    hear(5, 2)

    def part(q):
        return pl.ds(al(16 * q, 16), 16)

    for k in range(1, PLANE):
        t, q, _ = plane_peer(k, 1)
        remote(panel.at[part(q)], came_a.at[p], reduce_sem.at[0], reduce_sem.at[1], (t, ti)).start()
    came_a[p] = panel[part(p), :]

    local_pair.wait()
    mate_pair.wait_recv()
    pass_pair.wait_recv()
    row = place_ids(h, 0, 0, pair.shape)
    near[...] = jnp.where(row < size, pair[...].astype(F32), 0.0).astype(BF)
    which = lax.broadcasted_iota(jnp.int32, (128, 512), 0)
    wanted = jnp.where(which < 64, which + 64 * ti, which + (256 - 64) + 64 * ti)
    hot = jnp.where(lax.broadcasted_iota(jnp.int32, (128, 512), 1) == wanted, 1.0, 0.0).astype(BF)
    u = dot_nt(hot, near[...]).astype(BF)
    wide[pl.ds(0, 128), :] = first_step(dot(u, xh[...]) + dot(u, xl[...]))

    others_a = came_a.at[pl.ds(0, PLANE - 1)]
    drain(others_a, reduce_sem.at[1])
    total = came_a[0]
    for q in range(1, PLANE):
        total = total + came_a[q]
    piece[...] = total

    def tile_of(first, j):
        return pl.ds(al(first + 8 * (j // 4), 8), 8), pl.ds(al(128 * (j % 4), 128), 128)

    for k in sorted(range(1, z_count), key=lambda k: -min(k, z_count - k)):
        j = lax.rem(z + k, z_count) // 2
        remote(piece.at[tile_of(0, j)], came_z.at[z], reduce_sem.at[2], reduce_sem.at[3], z_device(k)).start()
    jz = z // 2
    tile_rows, tile_cols = tile_of(0, jz)
    came_z[z] = piece[tile_rows, tile_cols]
    cross_s = copy(start_hbm.at[:, near_cols], start_f.at[my_start, near_cols], cross, 4)
    mate_s = copy(start_hbm, start_f.at[my_start], mate, 4)

    v = wide[pl.ds(0, 128), :]
    w = product(product(v, kh[...], kl[...]), xh[...], xl[...])
    y_high, y_low = split(2.0 * v - first_step(w))
    to_near = dot(y_high, near[...]) + dot(y_low, near[...])
    to_glob = dot(y_high, g_perm[...]) + dot(y_low, g_perm[...])
    nxt[:, pl.ds(0, 256)] = to_near[0:64, 0:256]
    nxt[:, pl.ds(256, 512)] = to_glob[0:64, :]
    next_copy = copy(nxt, nxt_came, before, 5)
    off_out[...] = to_near[0:64, 256:512]
    diag_out[...] = to_near[64:128, 256:512]
    cross_out[...] = to_glob[64:128, :]
    local_base.wait()
    wide[...] = first_step(xh[mine, :].astype(F32) + xl[mine, :].astype(F32))

    others_z = came_z.at[pl.ds(0, z_count - 1)]
    drain(others_z, reduce_sem.at[3])
    total = came_z[0]
    for q in range(1, z_count):
        total = total + came_z[q]
    tile_rows, tile_cols = tile_of(16 * p, jz)
    own_piece = PLANE * ti + p
    tiles[own_piece, 0] = total + base[tile_rows, tile_cols]
    for k in sorted(range(2, z_count, 2), key=lambda k: -min(k, z_count - k)):
        at = COMES.index((z_count - k) // 2)
        late = 1 if at >= EARLY else 0
        here = tiles.at[own_piece, 0]
        remote(here, tiles.at[own_piece, at], reduce_sem.at[4], reduce_sem.at[9 + late], z_device(k)).start()

    def piece_of(hh, cc, q, wave):
        return tiles.at[PLANE * (2 * hh + cc) + q, pl.ds(0, EARLY) if wave == 0 else pl.ds(EARLY, 8 - EARLY)]

    order = (9, 10, 11, 12, 13, 14, 15, 2, 3, 4, 5, 6, 1, 7, 8)

    def spread(wave):
        here = piece_of(h, c, p, wave)
        came = []
        for k in order:
            made = remote(here, here, reduce_sem.at[6], recv_p.at[16 * wave + k], plane_device(k))
            made.start()
            came.append((k, made))
        remote(here, here, reduce_sem.at[7], reduce_sem.at[8], mate).start()
        return came

    def hand_over(came, wave):
        for k, made in came:
            made.wait_recv()
            _, q, hh = plane_peer(k, -1)
            ref = piece_of(hh, c, q, wave)
            remote(ref, ref, reduce_sem.at[7], reduce_sem.at[8], mate).start()

    v = wide[...]
    w = product(product(v, kh[...], kl[...]), xh[...], xl[...])
    drain(came_z.at[pl.ds(0, EARLY - 1)], reduce_sem.at[9])
    first_wave = spread(0)
    wide[...] = 2.0 * v - first_step(w)
    pass_s = hand_on(cross_s, start_f.at[cross_start, far_cols], 4)
    drain(came_z.at[pl.ds(0, 8 - EARLY)], reduce_sem.at[10])
    second_wave = spread(1)

    wide_high, wide_low = split(wide[...])
    yg = dot(wide_high, g_perm[...]) + dot(wide_low, g_perm[...])
    local_s.wait()
    mate_s.wait_recv()
    pass_s.wait_recv()
    start_f[far_cols, near_cols] = start_f[near_cols, far_cols].T
    s_high[...], s_low[...] = split(start_f[...])
    w_out[...] = product(yg, s_high[...], s_low[...])

    places = [lax.rem(jz + step, 8) for step in COMES]
    places = [(8 * (j // 4), al(128 * (j % 4), 128)) for j in places]

    def lay_out(cc, slots):
        def body(i, carry):
            q = PLANE * (2 * (i // PLANE) + cc) + lax.rem(i, PLANE)
            for at in slots:
                row, col = places[at]
                schur[pl.ds(al(16 * q + row, 8), 8), pl.ds(col, 128)] = tiles[q, at]
            return carry

        lax.fori_loop(0, 2 * PLANE, body, 0)

    hand_over(first_wave, 0)
    lay_out(c, range(EARLY))
    hand_over(second_wave, 1)
    lay_out(c, range(EARLY, 8))
    inner_out[...] = half_inner(c, w_out, schur)
    next_copy.wait_recv()
    last = jnp.where(tm == blocks - 1, 0.0, 1.0).astype(F32)
    diag_out[...] += nxt_came[:, pl.ds(0, 256)] * last
    cross_out[...] += nxt_came[:, pl.ds(256, 512)] * last
    others_p = schur.at[pl.ds(0, 16 * (2 * PLANE - 1))]
    everything = schur.at[pl.ds(0, 32 * PLANE)]
    drain(everything, reduce_sem.at[8])
    lay_out(1 - c, range(8))

    for group in range(4):
        drain(rows_x.at[pl.ds(0, 256)], send_sem.at[group])
    drain(start_f.at[pl.ds(0, 256)], send_sem.at[4])
    next_copy.wait_send()
    drain(others_a, reduce_sem.at[0])
    drain(others_z, reduce_sem.at[2])
    drain(came_z.at[pl.ds(0, z_count // 2 - 1)], reduce_sem.at[4])
    drain(others_p, reduce_sem.at[6])
    drain(everything, reduce_sem.at[7])


def half_inner(which, w, schur):
    first = pl.ds(al(128 * which, 128), 128)
    second = pl.ds(al(256 + 128 * which, 128), 128)
    t_high, t_low = split(jnp.concatenate([schur[first, :], schur[second, :]], axis=0))
    return product(jnp.concatenate([w[:, first], w[:, second]], axis=1), t_high, t_low)


def finish_kernel(
    diag, off, cross, schur, w, inner, s_high, s_low,
    diag_out, off_out, cross_out, schur_out, back_out,
    back, sem,
):
    mine = pl.ds(al(128 * lax.axis_index("tile"), 128), 128)
    pairs = ((diag, diag_out), (off, off_out), (cross, cross_out), (schur.at[mine], schur_out))
    copies = [pltpu.make_async_copy(a, b, sem.at[i]) for i, (a, b) in enumerate(pairs)]
    for made in copies:
        made.start()
    ti = lax.axis_index("tile")
    whole = inner[...] + half_inner(1 - lax.rem(ti, 2), w, schur)
    for i in range(2):
        rows = pl.ds(96 * i, 96)
        back[rows, :] = 2.0 * w[rows, :] - product(whole[96 * i : 96 * (i + 1)], s_high[...], s_low[...])
        made = pltpu.make_async_copy(back.at[rows], back_out.at[rows], sem.at[4 + i])
        made.start()
        copies.append(made)
    for made in copies:
        made.wait()


VM = pl.BlockSpec(memory_space=pltpu.VMEM)
SM = pl.BlockSpec(memory_space=pltpu.SMEM)
ANY = pl.BlockSpec(memory_space=pl.ANY)
HBM = pl.BlockSpec(memory_space=pltpu.HBM)
DMA = pltpu.SemaphoreType.DMA


def shards(operator, initial, block_sizes, link_index, link_pair, link_global, schur_base, schur_start):
    order = operator.shape[2]
    z_count = lax.axis_size("tm") // PLANE
    out = pl.pallas_call(
        functools.partial(block_kernel, z_count),
        out_shape=[
            pltpu.VMEM((64, 256), F32),
            pltpu.VMEM((64, 256), F32),
            pltpu.VMEM((64, 512), F32),
            pltpu.VMEM((512, 512), F32),
            pltpu.VMEM((ROWS, 512), F32),
            pltpu.VMEM((ROWS, 512), F32),
            pltpu.VMEM((512, 512), BF),
            pltpu.VMEM((512, 512), BF),
        ],
        in_specs=[SM] + [HBM] * 7,
        out_specs=[VM] * 8,
        scratch_shapes=[pltpu.VMEM((order, order), BF)] * 4
        + [pltpu.VMEM((HALF, order), F32)] * 2
        + [pltpu.VMEM((HALF, HALF), F32)] * 2
        + [
            pltpu.VMEM((order, 512), BF),
            pltpu.VMEM((order, 512), BF),
            pltpu.VMEM((1, 512), jnp.int32),
            pltpu.VMEM((128, 512), F32),
            pltpu.VMEM((128, 512), F32),
            pltpu.VMEM((PLANE, 16, 512), F32),
            pltpu.VMEM((16, 512), F32),
            pltpu.VMEM((z_count, 8, 128), F32),
            pltpu.VMEM((4 * PLANE, 8, 8, 128), F32),
            pltpu.VMEM((order, 512), BF),
            pltpu.VMEM((order, 512), BF),
            pltpu.VMEM((64, order), F32),
            pltpu.VMEM((64, order), F32),
            pltpu.VMEM((512, 512), F32),
            pltpu.VMEM((ROWS, order), F32),
            DMA((7,)),
            DMA((6,)),
            DMA((22,)),
            DMA((4 * PLANE,)),
            DMA((11,)),
            pltpu.SemaphoreType.REGULAR((6,)),
        ],
        compiler_params=pltpu.CompilerParams(collective_id=0, has_side_effects=True, vmem_limit_bytes=GRANT),
        name="block_step",
    )(
        block_sizes,
        *(
            pltpu.with_memory_space_constraint(array, pltpu.HBM)
            for array in (
                operator[0], initial[0], link_global[0], link_pair[0], link_index, schur_base, schur_start
            )
        ),
    )
    diag, off, cross, schur, back = pl.pallas_call(
        finish_kernel,
        out_shape=[
            jax.ShapeDtypeStruct((64, 256), F32),
            jax.ShapeDtypeStruct((64, 256), F32),
            jax.ShapeDtypeStruct((64, 512), F32),
            jax.ShapeDtypeStruct((128, 512), F32),
            jax.ShapeDtypeStruct((ROWS, 512), F32),
        ],
        in_specs=[VM] * 8,
        out_specs=[ANY] * 5,
        scratch_shapes=[pltpu.VMEM((ROWS, 512), F32), DMA((6,))],
        compiler_params=pltpu.CompilerParams(vmem_limit_bytes=GRANT),
        name="finish",
    )(*out)
    return diag[None], off[None], cross[None], schur, back[None]


def solution(mesh):
    return jax.shard_map(
        shards,
        mesh=mesh,
        in_specs=(
            P("tm", "tile", None),
            P("tm", "tile", None),
            P("tm"),
            P("tm", None),
            P("tm", "tile", None),
            P("tm", "tile", None),
            P("tile", None),
            P("tile", None),
        ),
        out_specs=(
            P("tm", "tile", None),
            P("tm", "tile", None),
            P("tm", "tile", None),
            P("tile", None),
            P("tm", "tile", None),
        ),
        check_vma=False,
    )
```

```python
import functools

import jax
import jax.numpy as jnp
from jax import lax
from jax.experimental import pallas as pl
from jax.experimental.pallas import tpu as pltpu
from jax.sharding import PartitionSpec as P

MESH = pl.DeviceIdType.MESH
BF = jnp.bfloat16
F32 = jnp.float32
PLANE = 8
HALF = 384
ROWS = 192
GRANT = 32 << 20
COMES = (0, 1, 2, 7, 6, 3, 4, 5)
EARLY = 5


def al(value, step):
    return pl.multiple_of(value, step)


def dot(left, right):
    return jnp.dot(left, right, preferred_element_type=F32)


def dot_nt(left, right):
    return lax.dot_general(left, right, (((1,), (1,)), ((), ())), preferred_element_type=F32)


def split(value):
    high = value.astype(BF)
    return high, (value - high.astype(F32)).astype(BF)


def product(value, high, low):
    value_high, value_low = split(value)
    rows = value.shape[0]
    if rows > 128:
        return dot(value_high, high) + dot(value_high, low) + dot(value_low, high)
    both = dot(jnp.concatenate([value_high, value_low], axis=0), high)
    return both[:rows] + both[rows:] + dot(value_high, low)


def position():
    tm = lax.axis_index("tm")
    ti = lax.axis_index("tile")
    h = ti // 2
    return tm, ti, h, ti - 2 * h


def remote(src, dst, send, recv, device):
    return pltpu.make_async_remote_copy(
        src_ref=src, dst_ref=dst, send_sem=send, recv_sem=recv, device_id=device, device_id_type=MESH
    )


def drain(ref, sem):
    pltpu.make_async_copy(ref, ref, sem).wait()


def greet(devices):
    barrier = pltpu.get_barrier_semaphore()
    for device in devices:
        pl.semaphore_signal(barrier, inc=1, device_id=device, device_id_type=MESH)


def place_ids(h, first, axis, shape):
    ids = lax.broadcasted_iota(jnp.int32, shape, axis) + first
    return jnp.where(ids < HALF, ids + h * HALF, ids - h * HALF)


def block_kernel(
    z_count,
    sizes, k_hbm, x_hbm, g_hbm, pair_hbm, index_hbm, base_hbm, start_hbm,
    diag_out, off_out, cross_out, schur, w_out, inner_out, s_high, s_low,
    xh, xl, kh, kl, rows_x, rows_k, diag_x, diag_k, rows_g, g_perm, index, base,
    panel, came_a, piece, came_z, tiles, pair, near, nxt, nxt_came, start_f, wide,
    local_sem, send_sem, recv_t, recv_p, reduce_sem, known,
):
    tm, ti, h, c = position()
    z = tm // PLANE
    p = tm - z * PLANE
    blocks = z_count * PLANE
    mate = (tm, ti + 1 - 2 * c)
    cross = (tm, lax.rem(ti + 2, 4))
    before = (lax.rem(tm + blocks - 1, blocks), ti)

    def plane_peer(k, sign):
        q = lax.rem(p + PLANE + sign * (k % PLANE), PLANE)
        return z * PLANE + q, q, lax.rem(h + k // PLANE, 2)

    def plane_device(k):
        t, q, hh = plane_peer(k, 1)
        return (t, 2 * hh + c)

    def z_device(k):
        return (lax.rem(z + k, z_count) * PLANE + p, ti)

    x_near = [plane_device(2), plane_device(PLANE - 2)]

    def z_near(by):
        return [z_device(by), z_device(z_count - by)]

    flip = p + 1 - 2 * lax.rem(p, 2)
    y_near = [(z * PLANE + flip, ti), (z * PLANE + flip, lax.rem(ti + 2, 4)), cross]
    greet(y_near + x_near + z_near(1) + [mate])

    def tell(round_, devices):
        for device in devices:
            pl.semaphore_signal(known.at[round_], inc=1, device_id=device, device_id_type=MESH)

    def hear(round_, count):
        pl.semaphore_wait(known.at[round_], count)

    own = al(h * HALF, 128)
    oth = al(HALF - h * HALF, 128)
    mine = pl.ds(al(ROWS * c, 64), ROWS)
    far = pl.ds(al(HALF + ROWS * c, 64), ROWS)
    my_start = pl.ds(al(128 * ti, 128), 128)
    cross_start = pl.ds(al(128 * lax.rem(ti + 2, 4), 128), 128)
    near_cols = pl.ds(al(256 * h, 256), 256)
    far_cols = pl.ds(al(256 - 256 * h, 256), 256)
    used = [0, 0]

    def slot(kind):
        used[kind] += 1
        return used[kind] - 1

    def copy(src, dst, device, group, at=None):
        made = remote(src, dst, send_sem.at[group], recv_t.at[slot(0) if at is None else at], device)
        made.start()
        return made

    def local(src, dst, at=None):
        made = pltpu.make_async_copy(src, dst, local_sem.at[slot(1) if at is None else at])
        made.start()
        return made

    def pieces(ref):
        return [
            ref.at[pl.ds(al(256 * c, 128), 128), pl.ds(al(256 * c, 128), 128)],
            ref.at[pl.ds(al(256 * c, 128), 128), pl.ds(al(128 - 128 * c, 128), 128)],
            ref.at[pl.ds(al(128 + 64 * c, 64), 64), pl.ds(128, 256)],
        ]

    def sources(hbm):
        return [
            hbm.at[pl.ds(al(64 * c, 64), 128), pl.ds(al(own + 256 * c, 128), 128)],
            hbm.at[pl.ds(al(64 * c, 64), 128), pl.ds(al(own + 128 - 128 * c, 128), 128)],
            hbm.at[pl.ds(al(128 - 128 * c, 64), 64), pl.ds(al(own + 128, 128), 256)],
        ]

    def halves(hbm, rows):
        return [
            (hbm.at[:, pl.ds(own, HALF)], rows.at[mine, pl.ds(0, HALF)]),
            (hbm.at[:, pl.ds(oth, HALF)], rows.at[mine, pl.ds(HALF, HALF)]),
        ]

    local_g = local(g_hbm, rows_g.at[mine])
    local_x, local_k = slot(1), slot(1)
    for src, dst in halves(x_hbm, rows_x):
        local(src, dst, local_x)
    for src, dst in halves(k_hbm, rows_k):
        local(src, dst, local_k)
    local_index = local(index_hbm, index)
    local_pair = local(pair_hbm, pair.at[mine])
    local_base = local(base_hbm, base)
    local_s = local(start_hbm, start_f.at[my_start])

    pl.semaphore_wait(pltpu.get_barrier_semaphore(), 8)

    cross_g = copy(g_hbm.at[:, far_cols], rows_g.at[far, far_cols], cross, 0)
    mate_g = copy(g_hbm, rows_g.at[mine], mate, 0)
    cross_x = [copy(a, b, cross, 1) for a, b in zip(sources(x_hbm), pieces(diag_x))]
    mate_x, mate_k, pass_x, pass_k = slot(0), slot(0), slot(0), slot(0)
    for src, dst in halves(x_hbm, rows_x):
        copy(src, dst, mate, 1, mate_x)
    cross_k = [copy(a, b, cross, 2) for a, b in zip(sources(k_hbm), pieces(diag_k))]
    for src, dst in halves(k_hbm, rows_k):
        copy(src, dst, mate, 2, mate_k)
    cross_g_rest = copy(g_hbm.at[:, near_cols], rows_g.at[far, near_cols], cross, 0)
    cross_pair = copy(pair_hbm, pair.at[far], cross, 0)
    mate_pair = copy(pair_hbm, pair.at[mine], mate, 0)
    tell(0, x_near)
    tell(1, z_near(1))

    def effective(block, first_row, first_col):
        row = place_ids(h, first_row, 0, block.shape)
        col = place_ids(h, first_col, 1, block.shape)
        unit = jnp.where(row == col, 1.0, 0.0).astype(F32)
        return jnp.where((row < size) & (col < size), block, unit)

    def store(high, low, row, col, value):
        n, m = value.shape
        value_high, value_low = split(value)
        high[pl.ds(row, n), pl.ds(col, m)] = value_high
        low[pl.ds(row, n), pl.ds(col, m)] = value_low

    def own_rows(rows, high, low):
        for i in range(3):
            at = 128 * i
            store(high, low, at, 0, effective(rows[pl.ds(at, 128), pl.ds(0, HALF)], at, 0))
            block = effective(rows[pl.ds(at, 128), pl.ds(HALF, HALF)], at, HALF)
            store(high, low, at, HALF, block)
            store(high, low, HALF, at, block.T)

    def far_rows(diag, high, low):
        for i in range(3):
            j = (i + 1) % 3
            at = HALF + 128 * i
            for col in (i, j):
                block = diag[pl.ds(128 * i, 128), pl.ds(128 * col, 128)]
                block = effective(block, at, HALF + 128 * col)
                store(high, low, at, HALF + 128 * col, block)
                if col == j:
                    store(high, low, HALF + 128 * j, at, block.T)

    def hand_on(came, ref, group=3, at=None):
        came.wait_recv()
        return copy(ref, ref, mate, group, at)

    lane = lax.broadcasted_iota(jnp.int32, (128, 128), 0)

    def permute(first):
        columns = pl.ds(first, 128)
        hot = jnp.where(lane == index[:, columns] - first, 1.0, 0.0).astype(BF)
        picked = dot(rows_g[:, columns], hot)
        return jnp.where(place_ids(h, 0, 0, picked.shape) < size, picked, 0.0)

    def first_step(u):
        return 2.0 * u - product(product(u, kh[...], kl[...]), xh[...], xl[...])

    size = sizes[0]
    local_index.wait()
    local_g.wait()
    mate_g.wait_recv()
    pass_g = hand_on(cross_g, rows_g.at[far, near_cols])
    hear(0, 2)
    hear(1, 2)
    tell(2, x_near)
    tell(3, z_near(2))
    drain(rows_x.at[mine], local_sem.at[local_x])
    drain(rows_x.at[mine], recv_t.at[mate_x])
    own_rows(rows_x, xh, xl)
    pass_g.wait_recv()
    u = permute(al(128 * ti, 128)).T.astype(BF)
    for made, ref in zip(cross_x, pieces(diag_x)):
        hand_on(made, ref, 3, pass_x)
    hear(2, 2)
    hear(3, 2)
    tell(4, z_near(1))
    tell(5, z_near(4))
    drain(rows_k.at[mine], local_sem.at[local_k])
    drain(rows_k.at[mine], recv_t.at[mate_k])
    own_rows(rows_k, kh, kl)
    drain(rows_x.at[pl.ds(0, 64)], recv_t.at[pass_x])
    far_rows(diag_x, xh, xl)
    v = dot(u, xh[...]) + dot(u, xl[...])
    w_own = product(v, kh[:, pl.ds(0, HALF)], kl[:, pl.ds(0, HALF)])
    first, second = pl.ds(0, HALF), pl.ds(HALF, HALF)
    w_far = product(v[:, :HALF], kh[first, second], kl[first, second])
    for made, ref in zip(cross_k, pieces(diag_k)):
        hand_on(made, ref, 3, pass_k)
    drain(rows_x.at[pl.ds(0, 64)], recv_t.at[pass_k])
    far_rows(diag_k, kh, kl)
    w_far = w_far + product(v[:, HALF:], kh[second, second], kl[second, second])
    v = 2.0 * v - product(jnp.concatenate([w_own, w_far], axis=1), xh[...], xl[...])
    pass_g_rest = hand_on(cross_g_rest, rows_g.at[far, far_cols])
    w = product(product(v, kh[...], kl[...]), xh[...], xl[...])
    pass_g_rest.wait_recv()
    for group in range(4):
        g_perm[:, pl.ds(128 * group, 128)] = permute(128 * group).astype(BF)
    y_high, y_low = split(2.0 * v - first_step(w))
    pass_pair = hand_on(cross_pair, pair.at[far])
    panel[...] = dot(y_high, g_perm[...]) + dot(y_low, g_perm[...])

    hear(4, 2)
    hear(5, 2)

    jz = z // 2
    steps = [lax.rem(jz + step, 8) for step in COMES]
    places = [(8 * (j // 4), al(128 * (j % 4), 128)) for j in steps]

    def tile_at(first, at):
        row, col = places[at]
        return pl.ds(al(first + row, 8), 8), pl.ds(col, 128)

    waves = ((range(EARLY, 8), 1), (range(EARLY), 5))
    for slots, sem in waves:
        for k in range(1, PLANE):
            t, q, _ = plane_peer(k, 1)
            for at in slots:
                src = panel.at[tile_at(16 * q, at)]
                remote(src, came_a.at[p, at], reduce_sem.at[0], reduce_sem.at[sem], (t, ti)).start()
    for at in range(8):
        rows, cols = tile_at(16 * p, at)
        came_a[p, at] = panel[rows, cols]

    local_pair.wait()
    mate_pair.wait_recv()
    pass_pair.wait_recv()
    row = place_ids(h, 0, 0, pair.shape)
    near[...] = jnp.where(row < size, pair[...].astype(F32), 0.0).astype(BF)
    which = lax.broadcasted_iota(jnp.int32, (128, 512), 0)
    wanted = jnp.where(which < 64, which + 64 * ti, which + (256 - 64) + 64 * ti)
    hot = jnp.where(lax.broadcasted_iota(jnp.int32, (128, 512), 1) == wanted, 1.0, 0.0).astype(BF)
    u = dot_nt(hot, near[...]).astype(BF)
    wide[pl.ds(0, 128), :] = first_step(dot(u, xh[...]) + dot(u, xl[...]))

    for slots, sem in waves:
        count = len(slots)
        span = pl.ds(slots[0], count)
        drain(came_a.at[pl.ds(0, PLANE - 1), span], reduce_sem.at[sem])
        total = came_a[0, span]
        for q in range(1, PLANE):
            total = total + came_a[q, span]
        piece[span] = total
        for at in sorted(slots, key=lambda at: -min(COMES[at], 8 - COMES[at])):
            for one in range(2):
                to = 2 * steps[at] + one
                if at == 0:
                    to = z + 1 - 2 * lax.rem(z, 2)
                if at or one:
                    device = (to * PLANE + p, ti)
                    remote(piece.at[at], came_z.at[z], reduce_sem.at[2], reduce_sem.at[3], device).start()
    came_z[z] = piece[0]
    others_a = came_a.at[pl.ds(0, PLANE - 1)]
    cross_s = copy(start_hbm.at[:, near_cols], start_f.at[my_start, near_cols], cross, 4)
    mate_s = copy(start_hbm, start_f.at[my_start], mate, 4)

    v = wide[pl.ds(0, 128), :]
    w = product(product(v, kh[...], kl[...]), xh[...], xl[...])
    y_high, y_low = split(2.0 * v - first_step(w))
    to_near = dot(y_high, near[...]) + dot(y_low, near[...])
    to_glob = dot(y_high, g_perm[...]) + dot(y_low, g_perm[...])
    nxt[:, pl.ds(0, 256)] = to_near[0:64, 0:256]
    nxt[:, pl.ds(256, 512)] = to_glob[0:64, :]
    next_copy = copy(nxt, nxt_came, before, 5)
    off_out[...] = to_near[0:64, 256:512]
    diag_out[...] = to_near[64:128, 256:512]
    cross_out[...] = to_glob[64:128, :]
    local_base.wait()
    wide[...] = first_step(xh[mine, :].astype(F32) + xl[mine, :].astype(F32))

    others_z = came_z.at[pl.ds(0, z_count - 1)]
    drain(others_z, reduce_sem.at[3])
    total = came_z[0]
    for q in range(1, z_count):
        total = total + came_z[q]
    tile_rows, tile_cols = tile_at(16 * p, 0)
    own_piece = PLANE * ti + p
    tiles[own_piece, 0] = total + base[tile_rows, tile_cols]
    for k in sorted(range(2, z_count, 2), key=lambda k: -min(k, z_count - k)):
        at = COMES.index((z_count - k) // 2)
        late = 1 if at >= EARLY else 0
        here = tiles.at[own_piece, 0]
        remote(here, tiles.at[own_piece, at], reduce_sem.at[4], reduce_sem.at[9 + late], z_device(k)).start()

    def piece_of(hh, cc, q, wave):
        return tiles.at[PLANE * (2 * hh + cc) + q, pl.ds(0, EARLY) if wave == 0 else pl.ds(EARLY, 8 - EARLY)]

    order = (9, 10, 11, 12, 13, 14, 15, 2, 3, 4, 5, 6, 1, 7, 8)

    def spread(wave):
        here = piece_of(h, c, p, wave)
        came = []
        for k in order:
            made = remote(here, here, reduce_sem.at[6], recv_p.at[16 * wave + k], plane_device(k))
            made.start()
            came.append((k, made))
        remote(here, here, reduce_sem.at[7], reduce_sem.at[8 + 3 * wave], mate).start()
        return came

    def hand_over(came, wave):
        for k, made in came:
            made.wait_recv()
            _, q, hh = plane_peer(k, -1)
            ref = piece_of(hh, c, q, wave)
            remote(ref, ref, reduce_sem.at[7], reduce_sem.at[8 + 3 * wave], mate).start()

    v = wide[...]
    w = product(product(v, kh[...], kl[...]), xh[...], xl[...])
    drain(came_z.at[pl.ds(0, EARLY - 1)], reduce_sem.at[9])
    first_wave = spread(0)
    wide[...] = 2.0 * v - first_step(w)
    pass_s = hand_on(cross_s, start_f.at[cross_start, far_cols], 4)
    drain(came_z.at[pl.ds(0, 8 - EARLY)], reduce_sem.at[10])
    second_wave = spread(1)

    wide_high, wide_low = split(wide[...])
    yg = dot(wide_high, g_perm[...]) + dot(wide_low, g_perm[...])
    local_s.wait()
    mate_s.wait_recv()
    pass_s.wait_recv()
    start_f[far_cols, near_cols] = start_f[near_cols, far_cols].T
    s_high[...], s_low[...] = split(start_f[...])
    w_out[...] = product(yg, s_high[...], s_low[...])

    def lay_out(cc, slots):
        def body(i, carry):
            q = PLANE * (2 * (i // PLANE) + cc) + lax.rem(i, PLANE)
            for at in slots:
                rows, cols = tile_at(16 * q, at)
                schur[rows, cols] = tiles[q, at]
            return carry

        lax.fori_loop(0, 2 * PLANE, body, 0)

    hand_over(first_wave, 0)
    lay_out(c, range(EARLY))
    hand_over(second_wave, 1)
    lay_out(c, range(EARLY, 8))
    inner_out[...] = half_inner(c, w_out, schur)
    next_copy.wait_recv()
    last = jnp.where(tm == blocks - 1, 0.0, 1.0).astype(F32)
    diag_out[...] += nxt_came[:, pl.ds(0, 256)] * last
    cross_out[...] += nxt_came[:, pl.ds(256, 512)] * last
    others_p = schur.at[pl.ds(0, 16 * (2 * PLANE - 1))]
    everything = schur.at[pl.ds(0, 32 * PLANE)]
    drain(tiles.at[pl.ds(0, 2 * PLANE), pl.ds(0, EARLY)], reduce_sem.at[8])
    lay_out(1 - c, range(EARLY))
    drain(tiles.at[pl.ds(0, 2 * PLANE), pl.ds(EARLY, 8 - EARLY)], reduce_sem.at[11])
    lay_out(1 - c, range(EARLY, 8))

    for group in range(4):
        drain(rows_x.at[pl.ds(0, 256)], send_sem.at[group])
    drain(start_f.at[pl.ds(0, 256)], send_sem.at[4])
    next_copy.wait_send()
    drain(others_a, reduce_sem.at[0])
    drain(others_z, reduce_sem.at[2])
    drain(came_z.at[pl.ds(0, z_count // 2 - 1)], reduce_sem.at[4])
    drain(others_p, reduce_sem.at[6])
    drain(everything, reduce_sem.at[7])


def half_inner(which, w, schur):
    first = pl.ds(al(128 * which, 128), 128)
    second = pl.ds(al(256 + 128 * which, 128), 128)
    t_high, t_low = split(jnp.concatenate([schur[first, :], schur[second, :]], axis=0))
    return product(jnp.concatenate([w[:, first], w[:, second]], axis=1), t_high, t_low)


def finish_kernel(
    diag, off, cross, schur, w, inner, s_high, s_low,
    diag_out, off_out, cross_out, schur_out, back_out,
    back, sem,
):
    mine = pl.ds(al(128 * lax.axis_index("tile"), 128), 128)
    pairs = ((diag, diag_out), (off, off_out), (cross, cross_out), (schur.at[mine], schur_out))
    copies = [pltpu.make_async_copy(a, b, sem.at[i]) for i, (a, b) in enumerate(pairs)]
    for made in copies:
        made.start()
    ti = lax.axis_index("tile")
    whole = inner[...] + half_inner(1 - lax.rem(ti, 2), w, schur)
    for i in range(2):
        rows = pl.ds(96 * i, 96)
        back[rows, :] = 2.0 * w[rows, :] - product(whole[96 * i : 96 * (i + 1)], s_high[...], s_low[...])
        made = pltpu.make_async_copy(back.at[rows], back_out.at[rows], sem.at[4 + i])
        made.start()
        copies.append(made)
    for made in copies:
        made.wait()


VM = pl.BlockSpec(memory_space=pltpu.VMEM)
SM = pl.BlockSpec(memory_space=pltpu.SMEM)
ANY = pl.BlockSpec(memory_space=pl.ANY)
HBM = pl.BlockSpec(memory_space=pltpu.HBM)
DMA = pltpu.SemaphoreType.DMA


def shards(operator, initial, block_sizes, link_index, link_pair, link_global, schur_base, schur_start):
    order = operator.shape[2]
    z_count = lax.axis_size("tm") // PLANE
    out = pl.pallas_call(
        functools.partial(block_kernel, z_count),
        out_shape=[
            pltpu.VMEM((64, 256), F32),
            pltpu.VMEM((64, 256), F32),
            pltpu.VMEM((64, 512), F32),
            pltpu.VMEM((512, 512), F32),
            pltpu.VMEM((ROWS, 512), F32),
            pltpu.VMEM((ROWS, 512), F32),
            pltpu.VMEM((512, 512), BF),
            pltpu.VMEM((512, 512), BF),
        ],
        in_specs=[SM] + [HBM] * 7,
        out_specs=[VM] * 8,
        scratch_shapes=[pltpu.VMEM((order, order), BF)] * 4
        + [pltpu.VMEM((HALF, order), F32)] * 2
        + [pltpu.VMEM((HALF, HALF), F32)] * 2
        + [
            pltpu.VMEM((order, 512), BF),
            pltpu.VMEM((order, 512), BF),
            pltpu.VMEM((1, 512), jnp.int32),
            pltpu.VMEM((128, 512), F32),
            pltpu.VMEM((128, 512), F32),
            pltpu.VMEM((PLANE, 8, 8, 128), F32),
            pltpu.VMEM((8, 8, 128), F32),
            pltpu.VMEM((z_count, 8, 128), F32),
            pltpu.VMEM((4 * PLANE, 8, 8, 128), F32),
            pltpu.VMEM((order, 512), BF),
            pltpu.VMEM((order, 512), BF),
            pltpu.VMEM((64, order), F32),
            pltpu.VMEM((64, order), F32),
            pltpu.VMEM((512, 512), F32),
            pltpu.VMEM((ROWS, order), F32),
            DMA((7,)),
            DMA((6,)),
            DMA((22,)),
            DMA((4 * PLANE,)),
            DMA((12,)),
            pltpu.SemaphoreType.REGULAR((6,)),
        ],
        compiler_params=pltpu.CompilerParams(collective_id=0, has_side_effects=True, vmem_limit_bytes=GRANT),
        name="block_step",
    )(
        block_sizes,
        *(
            pltpu.with_memory_space_constraint(array, pltpu.HBM)
            for array in (
                operator[0], initial[0], link_global[0], link_pair[0], link_index, schur_base, schur_start
            )
        ),
    )
    diag, off, cross, schur, back = pl.pallas_call(
        finish_kernel,
        out_shape=[
            jax.ShapeDtypeStruct((64, 256), F32),
            jax.ShapeDtypeStruct((64, 256), F32),
            jax.ShapeDtypeStruct((64, 512), F32),
            jax.ShapeDtypeStruct((128, 512), F32),
            jax.ShapeDtypeStruct((ROWS, 512), F32),
        ],
        in_specs=[VM] * 8,
        out_specs=[ANY] * 5,
        scratch_shapes=[pltpu.VMEM((ROWS, 512), F32), DMA((6,))],
        compiler_params=pltpu.CompilerParams(vmem_limit_bytes=GRANT),
        name="finish",
    )(*out)
    return diag[None], off[None], cross[None], schur, back[None]


def solution(mesh):
    return jax.shard_map(
        shards,
        mesh=mesh,
        in_specs=(
            P("tm", "tile", None),
            P("tm", "tile", None),
            P("tm"),
            P("tm", None),
            P("tm", "tile", None),
            P("tm", "tile", None),
            P("tile", None),
            P("tile", None),
        ),
        out_specs=(
            P("tm", "tile", None),
            P("tm", "tile", None),
            P("tm", "tile", None),
            P("tile", None),
            P("tm", "tile", None),
        ),
        check_vma=False,
    )
```

```python
import functools

import jax
import jax.numpy as jnp
from jax import lax
from jax.experimental import pallas as pl
from jax.experimental.pallas import tpu as pltpu
from jax.sharding import PartitionSpec as P

MESH = pl.DeviceIdType.MESH
BF = jnp.bfloat16
F32 = jnp.float32
PLANE = 8
HALF = 384
ROWS = 192
GRANT = 32 << 20
COMES = (0, 1, 2, 7, 6, 3, 4, 5)
EARLY = 5


def al(value, step):
    return pl.multiple_of(value, step)


def dot(left, right):
    return jnp.dot(left, right, preferred_element_type=F32)


def dot_nt(left, right):
    return lax.dot_general(left, right, (((1,), (1,)), ((), ())), preferred_element_type=F32)


def split(value):
    high = value.astype(BF)
    return high, (value - high.astype(F32)).astype(BF)


def product(value, high, low):
    value_high, value_low = split(value)
    rows = value.shape[0]
    if rows > 128:
        return dot(value_high, high) + dot(value_high, low) + dot(value_low, high)
    both = dot(jnp.concatenate([value_high, value_low], axis=0), high)
    return both[:rows] + both[rows:] + dot(value_high, low)


def position():
    tm = lax.axis_index("tm")
    ti = lax.axis_index("tile")
    h = ti // 2
    return tm, ti, h, ti - 2 * h


def remote(src, dst, send, recv, device):
    return pltpu.make_async_remote_copy(
        src_ref=src, dst_ref=dst, send_sem=send, recv_sem=recv, device_id=device, device_id_type=MESH
    )


def drain(ref, sem):
    pltpu.make_async_copy(ref, ref, sem).wait()


def greet(devices):
    barrier = pltpu.get_barrier_semaphore()
    for device in devices:
        pl.semaphore_signal(barrier, inc=1, device_id=device, device_id_type=MESH)


def place_ids(h, first, axis, shape):
    ids = lax.broadcasted_iota(jnp.int32, shape, axis) + first
    return jnp.where(ids < HALF, ids + h * HALF, ids - h * HALF)


def block_kernel(
    z_count,
    sizes, k_hbm, x_hbm, g_hbm, pair_hbm, index_hbm, base_hbm, start_hbm,
    diag_out, off_out, cross_out, schur, w_out, inner_out, s_high, s_low,
    xh, xl, kh, kl, rows_x, rows_k, diag_x, diag_k, rows_g, g_perm, index, base,
    panel, came_a, piece, came_z, tiles, pair, near, nxt, nxt_came, start_f, wide,
    local_sem, send_sem, recv_t, recv_p, reduce_sem, known,
):
    tm, ti, h, c = position()
    z = tm // PLANE
    p = tm - z * PLANE
    blocks = z_count * PLANE
    mate = (tm, ti + 1 - 2 * c)
    cross = (tm, lax.rem(ti + 2, 4))
    before = (lax.rem(tm + blocks - 1, blocks), ti)

    def plane_peer(k, sign):
        q = lax.rem(p + PLANE + sign * (k % PLANE), PLANE)
        return z * PLANE + q, q, lax.rem(h + k // PLANE, 2)

    def plane_device(k):
        t, q, hh = plane_peer(k, 1)
        return (t, 2 * hh + c)

    def z_device(k):
        return (lax.rem(z + k, z_count) * PLANE + p, ti)

    x_near = [plane_device(2), plane_device(PLANE - 2)]

    def z_near(by):
        return [z_device(by), z_device(z_count - by)]

    flip = p + 1 - 2 * lax.rem(p, 2)
    y_near = [(z * PLANE + flip, ti), (z * PLANE + flip, lax.rem(ti + 2, 4)), cross]
    greet(y_near + x_near + z_near(1) + [mate])

    def tell(round_, devices):
        for device in devices:
            pl.semaphore_signal(known.at[round_], inc=1, device_id=device, device_id_type=MESH)

    def hear(round_, count):
        pl.semaphore_wait(known.at[round_], count)

    own = al(h * HALF, 128)
    oth = al(HALF - h * HALF, 128)
    mine = pl.ds(al(ROWS * c, 64), ROWS)
    far = pl.ds(al(HALF + ROWS * c, 64), ROWS)
    my_start = pl.ds(al(128 * ti, 128), 128)
    cross_start = pl.ds(al(128 * lax.rem(ti + 2, 4), 128), 128)
    near_cols = pl.ds(al(256 * h, 256), 256)
    far_cols = pl.ds(al(256 - 256 * h, 256), 256)
    used = [0, 0]

    def slot(kind):
        used[kind] += 1
        return used[kind] - 1

    def copy(src, dst, device, group, at=None):
        made = remote(src, dst, send_sem.at[group], recv_t.at[slot(0) if at is None else at], device)
        made.start()
        return made

    def local(src, dst, at=None):
        made = pltpu.make_async_copy(src, dst, local_sem.at[slot(1) if at is None else at])
        made.start()
        return made

    def pieces(ref):
        return [
            ref.at[pl.ds(al(256 * c, 128), 128), pl.ds(al(256 * c, 128), 128)],
            ref.at[pl.ds(al(256 * c, 128), 128), pl.ds(al(128 - 128 * c, 128), 128)],
            ref.at[pl.ds(al(128 + 64 * c, 64), 64), pl.ds(128, 256)],
        ]

    def sources(hbm):
        return [
            hbm.at[pl.ds(al(64 * c, 64), 128), pl.ds(al(own + 256 * c, 128), 128)],
            hbm.at[pl.ds(al(64 * c, 64), 128), pl.ds(al(own + 128 - 128 * c, 128), 128)],
            hbm.at[pl.ds(al(128 - 128 * c, 64), 64), pl.ds(al(own + 128, 128), 256)],
        ]

    def halves(hbm, rows):
        return [
            (hbm.at[:, pl.ds(own, HALF)], rows.at[mine, pl.ds(0, HALF)]),
            (hbm.at[:, pl.ds(oth, HALF)], rows.at[mine, pl.ds(HALF, HALF)]),
        ]

    local_g = local(g_hbm, rows_g.at[mine])
    local_x, local_k = slot(1), slot(1)
    for src, dst in halves(x_hbm, rows_x):
        local(src, dst, local_x)
    for src, dst in halves(k_hbm, rows_k):
        local(src, dst, local_k)
    local_index = local(index_hbm, index)
    local_pair = local(pair_hbm, pair.at[mine])
    local_base = local(base_hbm, base)
    local_s = local(start_hbm, start_f.at[my_start])

    pl.semaphore_wait(pltpu.get_barrier_semaphore(), 8)

    cross_g = copy(g_hbm.at[:, far_cols], rows_g.at[far, far_cols], cross, 0)
    mate_g = copy(g_hbm, rows_g.at[mine], mate, 0)
    cross_x = [copy(a, b, cross, 1) for a, b in zip(sources(x_hbm), pieces(diag_x))]
    mate_x, mate_k, pass_x, pass_k = slot(0), slot(0), slot(0), slot(0)
    for src, dst in halves(x_hbm, rows_x):
        copy(src, dst, mate, 1, mate_x)
    cross_k = [copy(a, b, cross, 2) for a, b in zip(sources(k_hbm), pieces(diag_k))]
    for src, dst in halves(k_hbm, rows_k):
        copy(src, dst, mate, 2, mate_k)
    cross_g_rest = copy(g_hbm.at[:, near_cols], rows_g.at[far, near_cols], cross, 0)
    cross_pair = copy(pair_hbm, pair.at[far], cross, 0)
    mate_pair = copy(pair_hbm, pair.at[mine], mate, 0)
    tell(0, x_near)
    tell(1, z_near(1))

    def effective(block, first_row, first_col):
        row = place_ids(h, first_row, 0, block.shape)
        col = place_ids(h, first_col, 1, block.shape)
        unit = jnp.where(row == col, 1.0, 0.0).astype(F32)
        return jnp.where((row < size) & (col < size), block, unit)

    def store(high, low, row, col, value):
        n, m = value.shape
        value_high, value_low = split(value)
        high[pl.ds(row, n), pl.ds(col, m)] = value_high
        low[pl.ds(row, n), pl.ds(col, m)] = value_low

    def own_rows(rows, high, low):
        for i in range(3):
            at = 128 * i
            store(high, low, at, 0, effective(rows[pl.ds(at, 128), pl.ds(0, HALF)], at, 0))
            block = effective(rows[pl.ds(at, 128), pl.ds(HALF, HALF)], at, HALF)
            store(high, low, at, HALF, block)
            store(high, low, HALF, at, block.T)

    def far_rows(diag, high, low):
        for i in range(3):
            j = (i + 1) % 3
            at = HALF + 128 * i
            for col in (i, j):
                block = diag[pl.ds(128 * i, 128), pl.ds(128 * col, 128)]
                block = effective(block, at, HALF + 128 * col)
                store(high, low, at, HALF + 128 * col, block)
                if col == j:
                    store(high, low, HALF + 128 * j, at, block.T)

    def hand_on(came, ref, group=3, at=None):
        came.wait_recv()
        return copy(ref, ref, mate, group, at)

    lane = lax.broadcasted_iota(jnp.int32, (128, 128), 0)

    def permute(first):
        columns = pl.ds(first, 128)
        hot = jnp.where(lane == index[:, columns] - first, 1.0, 0.0).astype(BF)
        picked = dot(rows_g[:, columns], hot)
        return jnp.where(place_ids(h, 0, 0, picked.shape) < size, picked, 0.0)

    def first_step(u):
        return 2.0 * u - product(product(u, kh[...], kl[...]), xh[...], xl[...])

    size = sizes[0]
    local_index.wait()
    local_g.wait()
    mate_g.wait_recv()
    pass_g = hand_on(cross_g, rows_g.at[far, near_cols])
    hear(0, 2)
    hear(1, 2)
    tell(2, x_near)
    tell(3, z_near(2))
    drain(rows_x.at[mine], local_sem.at[local_x])
    drain(rows_x.at[mine], recv_t.at[mate_x])
    own_rows(rows_x, xh, xl)
    pass_g.wait_recv()
    u = permute(al(128 * ti, 128)).T.astype(BF)
    for made, ref in zip(cross_x, pieces(diag_x)):
        hand_on(made, ref, 3, pass_x)
    hear(2, 2)
    hear(3, 2)
    tell(4, z_near(1))
    tell(5, z_near(4))
    drain(rows_k.at[mine], local_sem.at[local_k])
    drain(rows_k.at[mine], recv_t.at[mate_k])
    own_rows(rows_k, kh, kl)
    drain(rows_x.at[pl.ds(0, 64)], recv_t.at[pass_x])
    far_rows(diag_x, xh, xl)
    v = dot(u, xh[...]) + dot(u, xl[...])
    w_own = product(v, kh[:, pl.ds(0, HALF)], kl[:, pl.ds(0, HALF)])
    first, second = pl.ds(0, HALF), pl.ds(HALF, HALF)
    w_far = product(v[:, :HALF], kh[first, second], kl[first, second])
    for i in range(2):
        at = al(256 * h + 128 * i, 128)
        g_perm[:, pl.ds(at, 128)] = permute(at).astype(BF)
    for made, ref in zip(cross_k, pieces(diag_k)):
        hand_on(made, ref, 3, pass_k)
    drain(rows_x.at[pl.ds(0, 64)], recv_t.at[pass_k])
    far_rows(diag_k, kh, kl)
    w_far = w_far + product(v[:, HALF:], kh[second, second], kl[second, second])
    v = 2.0 * v - product(jnp.concatenate([w_own, w_far], axis=1), xh[...], xl[...])
    pass_g_rest = hand_on(cross_g_rest, rows_g.at[far, far_cols])
    w = product(product(v, kh[...], kl[...]), xh[...], xl[...])
    pass_g_rest.wait_recv()
    for i in range(2):
        at = al(256 - 256 * h + 128 * i, 128)
        g_perm[:, pl.ds(at, 128)] = permute(at).astype(BF)
    y_high, y_low = split(2.0 * v - first_step(w))
    pass_pair = hand_on(cross_pair, pair.at[far])
    panel[...] = dot(y_high, g_perm[...]) + dot(y_low, g_perm[...])

    hear(4, 2)
    hear(5, 2)

    jz = z // 2
    steps = [lax.rem(jz + step, 8) for step in COMES]
    places = [(8 * (j // 4), al(128 * (j % 4), 128)) for j in steps]

    def tile_at(first, at):
        row, col = places[at]
        return pl.ds(al(first + row, 8), 8), pl.ds(col, 128)

    waves = ((range(EARLY, 8), 1), (range(EARLY), 5))
    for slots, sem in waves:
        for k in range(1, PLANE):
            t, q, _ = plane_peer(k, 1)
            for at in slots:
                src = panel.at[tile_at(16 * q, at)]
                remote(src, came_a.at[p, at], reduce_sem.at[0], reduce_sem.at[sem], (t, ti)).start()
    for at in range(8):
        rows, cols = tile_at(16 * p, at)
        came_a[p, at] = panel[rows, cols]

    local_pair.wait()
    mate_pair.wait_recv()
    pass_pair.wait_recv()
    row = place_ids(h, 0, 0, pair.shape)
    near[...] = jnp.where(row < size, pair[...].astype(F32), 0.0).astype(BF)
    which = lax.broadcasted_iota(jnp.int32, (128, 512), 0)
    wanted = jnp.where(which < 64, which + 64 * ti, which + (256 - 64) + 64 * ti)
    hot = jnp.where(lax.broadcasted_iota(jnp.int32, (128, 512), 1) == wanted, 1.0, 0.0).astype(BF)
    u = dot_nt(hot, near[...]).astype(BF)
    wide[pl.ds(0, 128), :] = first_step(dot(u, xh[...]) + dot(u, xl[...]))

    for slots, sem in waves:
        count = len(slots)
        span = pl.ds(slots[0], count)
        drain(came_a.at[pl.ds(0, PLANE - 1), span], reduce_sem.at[sem])
        total = came_a[0, span]
        for q in range(1, PLANE):
            total = total + came_a[q, span]
        piece[span] = total
        for at in sorted(slots, key=lambda at: -min(COMES[at], 8 - COMES[at])):
            for one in range(2):
                to = 2 * steps[at] + one
                if at == 0:
                    to = z + 1 - 2 * lax.rem(z, 2)
                if at or one:
                    device = (to * PLANE + p, ti)
                    remote(piece.at[at], came_z.at[z], reduce_sem.at[2], reduce_sem.at[3], device).start()
    came_z[z] = piece[0]
    others_a = came_a.at[pl.ds(0, PLANE - 1)]
    cross_s = copy(start_hbm.at[:, near_cols], start_f.at[my_start, near_cols], cross, 4)
    mate_s = copy(start_hbm, start_f.at[my_start], mate, 4)

    v = wide[pl.ds(0, 128), :]
    w = product(product(v, kh[...], kl[...]), xh[...], xl[...])
    y_high, y_low = split(2.0 * v - first_step(w))
    to_near = dot(y_high, near[...]) + dot(y_low, near[...])
    to_glob = dot(y_high, g_perm[...]) + dot(y_low, g_perm[...])
    nxt[:, pl.ds(0, 256)] = to_near[0:64, 0:256]
    nxt[:, pl.ds(256, 512)] = to_glob[0:64, :]
    next_copy = copy(nxt, nxt_came, before, 5)
    off_out[...] = to_near[0:64, 256:512]
    diag_out[...] = to_near[64:128, 256:512]
    cross_out[...] = to_glob[64:128, :]
    local_base.wait()
    own_x = xh[mine, :].astype(F32) + xl[mine, :].astype(F32)
    wide[...] = product(own_x, kh[...], kl[...])

    others_z = came_z.at[pl.ds(0, z_count - 1)]
    drain(others_z, reduce_sem.at[3])
    total = came_z[0]
    for q in range(1, z_count):
        total = total + came_z[q]
    tile_rows, tile_cols = tile_at(16 * p, 0)
    own_piece = PLANE * ti + p
    tiles[own_piece, 0] = total + base[tile_rows, tile_cols]
    for k in sorted(range(2, z_count, 2), key=lambda k: -min(k, z_count - k)):
        at = COMES.index((z_count - k) // 2)
        late = 1 if at >= EARLY else 0
        here = tiles.at[own_piece, 0]
        remote(here, tiles.at[own_piece, at], reduce_sem.at[4], reduce_sem.at[9 + late], z_device(k)).start()

    def piece_of(hh, cc, q, wave):
        return tiles.at[PLANE * (2 * hh + cc) + q, pl.ds(0, EARLY) if wave == 0 else pl.ds(EARLY, 8 - EARLY)]

    order = (9, 10, 11, 12, 13, 14, 15, 2, 3, 4, 5, 6, 1, 7, 8)

    def spread(wave):
        here = piece_of(h, c, p, wave)
        came = []
        for k in order:
            made = remote(here, here, reduce_sem.at[6], recv_p.at[16 * wave + k], plane_device(k))
            made.start()
            came.append((k, made))
        remote(here, here, reduce_sem.at[7], reduce_sem.at[8 + 3 * wave], mate).start()
        return came

    def hand_over(came, wave):
        for k, made in came:
            made.wait_recv()
            _, q, hh = plane_peer(k, -1)
            ref = piece_of(hh, c, q, wave)
            remote(ref, ref, reduce_sem.at[7], reduce_sem.at[8 + 3 * wave], mate).start()

    own_x = xh[mine, :].astype(F32) + xl[mine, :].astype(F32)
    v = 2.0 * own_x - product(wide[...], xh[...], xl[...])
    w = product(product(v, kh[...], kl[...]), xh[...], xl[...])
    drain(came_z.at[pl.ds(0, EARLY - 1)], reduce_sem.at[9])
    first_wave = spread(0)
    wide[...] = 2.0 * v - first_step(w)
    pass_s = hand_on(cross_s, start_f.at[cross_start, far_cols], 4)
    drain(came_z.at[pl.ds(0, 8 - EARLY)], reduce_sem.at[10])
    second_wave = spread(1)

    wide_high, wide_low = split(wide[...])
    yg = dot(wide_high, g_perm[...]) + dot(wide_low, g_perm[...])
    local_s.wait()
    mate_s.wait_recv()
    pass_s.wait_recv()
    start_f[far_cols, near_cols] = start_f[near_cols, far_cols].T
    s_high[...], s_low[...] = split(start_f[...])
    w_out[...] = product(yg, s_high[...], s_low[...])

    def lay_out(cc, slots):
        def body(i, carry):
            q = PLANE * (2 * (i // PLANE) + cc) + lax.rem(i, PLANE)
            for at in slots:
                rows, cols = tile_at(16 * q, at)
                schur[rows, cols] = tiles[q, at]
            return carry

        lax.fori_loop(0, 2 * PLANE, body, 0)

    hand_over(first_wave, 0)
    lay_out(c, range(EARLY))
    hand_over(second_wave, 1)
    lay_out(c, range(EARLY, 8))
    inner_out[...] = half_inner(c, w_out, schur)
    next_copy.wait_recv()
    last = jnp.where(tm == blocks - 1, 0.0, 1.0).astype(F32)
    diag_out[...] += nxt_came[:, pl.ds(0, 256)] * last
    cross_out[...] += nxt_came[:, pl.ds(256, 512)] * last
    others_p = schur.at[pl.ds(0, 16 * (2 * PLANE - 1))]
    everything = schur.at[pl.ds(0, 32 * PLANE)]
    drain(tiles.at[pl.ds(0, 2 * PLANE), pl.ds(0, EARLY)], reduce_sem.at[8])
    lay_out(1 - c, range(EARLY))
    drain(tiles.at[pl.ds(0, 2 * PLANE), pl.ds(EARLY, 8 - EARLY)], reduce_sem.at[11])
    lay_out(1 - c, range(EARLY, 8))

    for group in range(4):
        drain(rows_x.at[pl.ds(0, 256)], send_sem.at[group])
    drain(start_f.at[pl.ds(0, 256)], send_sem.at[4])
    next_copy.wait_send()
    drain(others_a, reduce_sem.at[0])
    drain(others_z, reduce_sem.at[2])
    drain(came_z.at[pl.ds(0, z_count // 2 - 1)], reduce_sem.at[4])
    drain(others_p, reduce_sem.at[6])
    drain(everything, reduce_sem.at[7])


def half_inner(which, w, schur):
    first = pl.ds(al(128 * which, 128), 128)
    second = pl.ds(al(256 + 128 * which, 128), 128)
    t_high, t_low = split(jnp.concatenate([schur[first, :], schur[second, :]], axis=0))
    return product(jnp.concatenate([w[:, first], w[:, second]], axis=1), t_high, t_low)


def finish_kernel(
    diag, off, cross, schur, w, inner, s_high, s_low,
    diag_out, off_out, cross_out, schur_out, back_out,
    back, sem,
):
    mine = pl.ds(al(128 * lax.axis_index("tile"), 128), 128)
    pairs = ((diag, diag_out), (off, off_out), (cross, cross_out), (schur.at[mine], schur_out))
    copies = [pltpu.make_async_copy(a, b, sem.at[i]) for i, (a, b) in enumerate(pairs)]
    for made in copies:
        made.start()
    ti = lax.axis_index("tile")
    whole = inner[...] + half_inner(1 - lax.rem(ti, 2), w, schur)
    for i in range(2):
        rows = pl.ds(96 * i, 96)
        back[rows, :] = 2.0 * w[rows, :] - product(whole[96 * i : 96 * (i + 1)], s_high[...], s_low[...])
        made = pltpu.make_async_copy(back.at[rows], back_out.at[rows], sem.at[4 + i])
        made.start()
        copies.append(made)
    for made in copies:
        made.wait()


VM = pl.BlockSpec(memory_space=pltpu.VMEM)
SM = pl.BlockSpec(memory_space=pltpu.SMEM)
ANY = pl.BlockSpec(memory_space=pl.ANY)
HBM = pl.BlockSpec(memory_space=pltpu.HBM)
DMA = pltpu.SemaphoreType.DMA


def shards(operator, initial, block_sizes, link_index, link_pair, link_global, schur_base, schur_start):
    order = operator.shape[2]
    z_count = lax.axis_size("tm") // PLANE
    out = pl.pallas_call(
        functools.partial(block_kernel, z_count),
        out_shape=[
            pltpu.VMEM((64, 256), F32),
            pltpu.VMEM((64, 256), F32),
            pltpu.VMEM((64, 512), F32),
            pltpu.VMEM((512, 512), F32),
            pltpu.VMEM((ROWS, 512), F32),
            pltpu.VMEM((ROWS, 512), F32),
            pltpu.VMEM((512, 512), BF),
            pltpu.VMEM((512, 512), BF),
        ],
        in_specs=[SM] + [HBM] * 7,
        out_specs=[VM] * 8,
        scratch_shapes=[pltpu.VMEM((order, order), BF)] * 4
        + [pltpu.VMEM((HALF, order), F32)] * 2
        + [pltpu.VMEM((HALF, HALF), F32)] * 2
        + [
            pltpu.VMEM((order, 512), BF),
            pltpu.VMEM((order, 512), BF),
            pltpu.VMEM((1, 512), jnp.int32),
            pltpu.VMEM((128, 512), F32),
            pltpu.VMEM((128, 512), F32),
            pltpu.VMEM((PLANE, 8, 8, 128), F32),
            pltpu.VMEM((8, 8, 128), F32),
            pltpu.VMEM((z_count, 8, 128), F32),
            pltpu.VMEM((4 * PLANE, 8, 8, 128), F32),
            pltpu.VMEM((order, 512), BF),
            pltpu.VMEM((order, 512), BF),
            pltpu.VMEM((64, order), F32),
            pltpu.VMEM((64, order), F32),
            pltpu.VMEM((512, 512), F32),
            pltpu.VMEM((ROWS, order), F32),
            DMA((7,)),
            DMA((6,)),
            DMA((22,)),
            DMA((4 * PLANE,)),
            DMA((12,)),
            pltpu.SemaphoreType.REGULAR((6,)),
        ],
        compiler_params=pltpu.CompilerParams(collective_id=0, has_side_effects=True, vmem_limit_bytes=GRANT),
        name="block_step",
    )(
        block_sizes,
        *(
            pltpu.with_memory_space_constraint(array, pltpu.HBM)
            for array in (
                operator[0], initial[0], link_global[0], link_pair[0], link_index, schur_base, schur_start
            )
        ),
    )
    diag, off, cross, schur, back = pl.pallas_call(
        finish_kernel,
        out_shape=[
            jax.ShapeDtypeStruct((64, 256), F32),
            jax.ShapeDtypeStruct((64, 256), F32),
            jax.ShapeDtypeStruct((64, 512), F32),
            jax.ShapeDtypeStruct((128, 512), F32),
            jax.ShapeDtypeStruct((ROWS, 512), F32),
        ],
        in_specs=[VM] * 8,
        out_specs=[ANY] * 5,
        scratch_shapes=[pltpu.VMEM((ROWS, 512), F32), DMA((6,))],
        compiler_params=pltpu.CompilerParams(vmem_limit_bytes=GRANT),
        name="finish",
    )(*out)
    return diag[None], off[None], cross[None], schur, back[None]


def solution(mesh):
    return jax.shard_map(
        shards,
        mesh=mesh,
        in_specs=(
            P("tm", "tile", None),
            P("tm", "tile", None),
            P("tm"),
            P("tm", None),
            P("tm", "tile", None),
            P("tm", "tile", None),
            P("tile", None),
            P("tile", None),
        ),
        out_specs=(
            P("tm", "tile", None),
            P("tm", "tile", None),
            P("tm", "tile", None),
            P("tile", None),
            P("tm", "tile", None),
        ),
        check_vma=False,
    )
```

```python
import functools

import jax
import jax.numpy as jnp
from jax import lax
from jax.experimental import pallas as pl
from jax.experimental.pallas import tpu as pltpu
from jax.sharding import PartitionSpec as P

MESH = pl.DeviceIdType.MESH
BF = jnp.bfloat16
F32 = jnp.float32
PLANE = 8
HALF = 384
ROWS = 192
GRANT = 32 << 20
COMES = (0, 1, 2, 7, 6, 3, 4, 5)
EARLY = 5


def al(value, step):
    return pl.multiple_of(value, step)


def dot(left, right):
    return jnp.dot(left, right, preferred_element_type=F32)


def dot_nt(left, right):
    return lax.dot_general(left, right, (((1,), (1,)), ((), ())), preferred_element_type=F32)


def split(value):
    high = value.astype(BF)
    return high, (value - high.astype(F32)).astype(BF)


def product(value, high, low):
    value_high, value_low = split(value)
    rows = value.shape[0]
    if rows > 128:
        return dot(value_high, high) + dot(value_high, low) + dot(value_low, high)
    both = dot(jnp.concatenate([value_high, value_low], axis=0), high)
    return both[:rows] + both[rows:] + dot(value_high, low)


def position():
    tm = lax.axis_index("tm")
    ti = lax.axis_index("tile")
    h = ti // 2
    return tm, ti, h, ti - 2 * h


def remote(src, dst, send, recv, device):
    return pltpu.make_async_remote_copy(
        src_ref=src, dst_ref=dst, send_sem=send, recv_sem=recv, device_id=device, device_id_type=MESH
    )


def drain(ref, sem):
    pltpu.make_async_copy(ref, ref, sem).wait()


def greet(devices):
    barrier = pltpu.get_barrier_semaphore()
    for device in devices:
        pl.semaphore_signal(barrier, inc=1, device_id=device, device_id_type=MESH)


def place_ids(h, first, axis, shape):
    ids = lax.broadcasted_iota(jnp.int32, shape, axis) + first
    return jnp.where(ids < HALF, ids + h * HALF, ids - h * HALF)


def block_kernel(
    z_count,
    sizes, k_hbm, x_hbm, g_hbm, pair_hbm, index_hbm, base_hbm, start_hbm,
    diag_out, off_out, cross_out, schur, w_out, inner_out, s_high, s_low,
    xh, xl, kh, kl, rows_x, rows_k, diag_x, diag_k, rows_g, g_perm, index, base,
    panel, came_a, piece, came_z, tiles, pair, near, nxt, nxt_came, start_f, wide,
    local_sem, send_sem, recv_t, recv_p, reduce_sem, known,
):
    tm, ti, h, c = position()
    z = tm // PLANE
    p = tm - z * PLANE
    blocks = z_count * PLANE
    mate = (tm, ti + 1 - 2 * c)
    cross = (tm, lax.rem(ti + 2, 4))
    before = (lax.rem(tm + blocks - 1, blocks), ti)

    def plane_peer(k, sign):
        q = lax.rem(p + PLANE + sign * (k % PLANE), PLANE)
        return z * PLANE + q, q, lax.rem(h + k // PLANE, 2)

    def plane_device(k):
        t, q, hh = plane_peer(k, 1)
        return (t, 2 * hh + c)

    def z_device(k):
        return (lax.rem(z + k, z_count) * PLANE + p, ti)

    x_near = [plane_device(2), plane_device(PLANE - 2)]

    def z_near(by):
        return [z_device(by), z_device(z_count - by)]

    flip = p + 1 - 2 * lax.rem(p, 2)
    y_near = [(z * PLANE + flip, ti), (z * PLANE + flip, lax.rem(ti + 2, 4)), cross]
    greet(y_near + x_near + z_near(1) + [mate])

    def tell(round_, devices):
        for device in devices:
            pl.semaphore_signal(known.at[round_], inc=1, device_id=device, device_id_type=MESH)

    def hear(round_, count):
        pl.semaphore_wait(known.at[round_], count)

    own = al(h * HALF, 128)
    oth = al(HALF - h * HALF, 128)
    mine = pl.ds(al(ROWS * c, 64), ROWS)
    far = pl.ds(al(HALF + ROWS * c, 64), ROWS)
    my_start = pl.ds(al(128 * ti, 128), 128)
    cross_start = pl.ds(al(128 * lax.rem(ti + 2, 4), 128), 128)
    near_cols = pl.ds(al(256 * h, 256), 256)
    far_cols = pl.ds(al(256 - 256 * h, 256), 256)
    used = [0, 0]

    def slot(kind):
        used[kind] += 1
        return used[kind] - 1

    def copy(src, dst, device, group, at=None):
        made = remote(src, dst, send_sem.at[group], recv_t.at[slot(0) if at is None else at], device)
        made.start()
        return made

    def local(src, dst, at=None):
        made = pltpu.make_async_copy(src, dst, local_sem.at[slot(1) if at is None else at])
        made.start()
        return made

    def pieces(ref):
        return [
            ref.at[pl.ds(al(256 * c, 128), 128), pl.ds(al(256 * c, 128), 128)],
            ref.at[pl.ds(al(256 * c, 128), 128), pl.ds(al(128 - 128 * c, 128), 128)],
            ref.at[pl.ds(al(128 + 64 * c, 64), 64), pl.ds(128, 256)],
        ]

    def sources(hbm):
        return [
            hbm.at[pl.ds(al(64 * c, 64), 128), pl.ds(al(own + 256 * c, 128), 128)],
            hbm.at[pl.ds(al(64 * c, 64), 128), pl.ds(al(own + 128 - 128 * c, 128), 128)],
            hbm.at[pl.ds(al(128 - 128 * c, 64), 64), pl.ds(al(own + 128, 128), 256)],
        ]

    def halves(hbm, rows):
        return [
            (hbm.at[:, pl.ds(own, HALF)], rows.at[mine, pl.ds(0, HALF)]),
            (hbm.at[:, pl.ds(oth, HALF)], rows.at[mine, pl.ds(HALF, HALF)]),
        ]

    local_g = local(g_hbm, rows_g.at[mine])
    local_x, local_k = slot(1), slot(1)
    for src, dst in halves(x_hbm, rows_x):
        local(src, dst, local_x)
    for src, dst in halves(k_hbm, rows_k):
        local(src, dst, local_k)
    local_index = local(index_hbm, index)
    local_pair = local(pair_hbm, pair.at[mine])
    local_base = local(base_hbm, base)
    local_s = local(start_hbm, start_f.at[my_start])

    pl.semaphore_wait(pltpu.get_barrier_semaphore(), 8)

    cross_g = copy(g_hbm.at[:, far_cols], rows_g.at[far, far_cols], cross, 0)
    mate_g = copy(g_hbm, rows_g.at[mine], mate, 0)
    cross_x = [copy(a, b, cross, 1) for a, b in zip(sources(x_hbm), pieces(diag_x))]
    mate_x, mate_k, pass_x, pass_k = slot(0), slot(0), slot(0), slot(0)
    for src, dst in halves(x_hbm, rows_x):
        copy(src, dst, mate, 1, mate_x)
    cross_k = [copy(a, b, cross, 2) for a, b in zip(sources(k_hbm), pieces(diag_k))]
    for src, dst in halves(k_hbm, rows_k):
        copy(src, dst, mate, 2, mate_k)
    cross_g_rest = copy(g_hbm.at[:, near_cols], rows_g.at[far, near_cols], cross, 0)
    cross_pair = copy(pair_hbm, pair.at[far], cross, 0)
    mate_pair = copy(pair_hbm, pair.at[mine], mate, 0)
    tell(0, x_near)
    tell(1, z_near(1))

    def effective(block, first_row, first_col):
        row = place_ids(h, first_row, 0, block.shape)
        col = place_ids(h, first_col, 1, block.shape)
        unit = jnp.where(row == col, 1.0, 0.0).astype(F32)
        return jnp.where((row < size) & (col < size), block, unit)

    def store(high, low, row, col, value):
        n, m = value.shape
        value_high, value_low = split(value)
        high[pl.ds(row, n), pl.ds(col, m)] = value_high
        low[pl.ds(row, n), pl.ds(col, m)] = value_low

    def own_rows(rows, high, low):
        for i in range(3):
            at = 128 * i
            store(high, low, at, 0, effective(rows[pl.ds(at, 128), pl.ds(0, HALF)], at, 0))
            block = effective(rows[pl.ds(at, 128), pl.ds(HALF, HALF)], at, HALF)
            store(high, low, at, HALF, block)
            store(high, low, HALF, at, block.T)

    def far_rows(diag, high, low):
        for i in range(3):
            j = (i + 1) % 3
            at = HALF + 128 * i
            for col in (i, j):
                block = diag[pl.ds(128 * i, 128), pl.ds(128 * col, 128)]
                block = effective(block, at, HALF + 128 * col)
                store(high, low, at, HALF + 128 * col, block)
                if col == j:
                    store(high, low, HALF + 128 * j, at, block.T)

    def hand_on(came, ref, group=3, at=None):
        came.wait_recv()
        return copy(ref, ref, mate, group, at)

    lane = lax.broadcasted_iota(jnp.int32, (128, 128), 0)

    def permute(first):
        columns = pl.ds(first, 128)
        hot = jnp.where(lane == index[:, columns] - first, 1.0, 0.0).astype(BF)
        picked = dot(rows_g[:, columns], hot)
        return jnp.where(place_ids(h, 0, 0, picked.shape) < size, picked, 0.0)

    def first_step(u):
        return 2.0 * u - product(product(u, kh[...], kl[...]), xh[...], xl[...])

    size = sizes[0]
    local_index.wait()
    local_g.wait()
    mate_g.wait_recv()
    pass_g = hand_on(cross_g, rows_g.at[far, near_cols])
    hear(0, 2)
    hear(1, 2)
    tell(2, x_near)
    tell(3, z_near(2))
    drain(rows_x.at[mine], local_sem.at[local_x])
    drain(rows_x.at[mine], recv_t.at[mate_x])
    own_rows(rows_x, xh, xl)
    pass_g.wait_recv()
    u = permute(al(128 * ti, 128)).T.astype(BF)
    for made, ref in zip(cross_x, pieces(diag_x)):
        hand_on(made, ref, 3, pass_x)
    hear(2, 2)
    hear(3, 2)
    tell(4, z_near(1))
    tell(5, z_near(4))
    drain(rows_k.at[mine], local_sem.at[local_k])
    drain(rows_k.at[mine], recv_t.at[mate_k])
    own_rows(rows_k, kh, kl)
    drain(rows_x.at[pl.ds(0, 64)], recv_t.at[pass_x])
    far_rows(diag_x, xh, xl)
    v = dot(u, xh[...]) + dot(u, xl[...])
    w_own = product(v, kh[:, pl.ds(0, HALF)], kl[:, pl.ds(0, HALF)])
    first, second = pl.ds(0, HALF), pl.ds(HALF, HALF)
    w_far = product(v[:, :HALF], kh[first, second], kl[first, second])
    for i in range(2):
        at = al(256 * h + 128 * i, 128)
        g_perm[:, pl.ds(at, 128)] = permute(at).astype(BF)
    for made, ref in zip(cross_k, pieces(diag_k)):
        hand_on(made, ref, 3, pass_k)
    drain(rows_x.at[pl.ds(0, 64)], recv_t.at[pass_k])
    far_rows(diag_k, kh, kl)
    w_far = w_far + product(v[:, HALF:], kh[second, second], kl[second, second])
    v = 2.0 * v - product(jnp.concatenate([w_own, w_far], axis=1), xh[...], xl[...])
    pass_g_rest = hand_on(cross_g_rest, rows_g.at[far, far_cols])
    w = product(product(v, kh[...], kl[...]), xh[...], xl[...])
    pass_g_rest.wait_recv()
    for i in range(2):
        at = al(256 - 256 * h + 128 * i, 128)
        g_perm[:, pl.ds(at, 128)] = permute(at).astype(BF)
    y_high, y_low = split(2.0 * v - first_step(w))
    pass_pair = hand_on(cross_pair, pair.at[far])
    panel[...] = dot(y_high, g_perm[...]) + dot(y_low, g_perm[...])

    hear(4, 2)
    hear(5, 2)

    jz = z // 2
    steps = [lax.rem(jz + step, 8) for step in COMES]
    places = [(8 * (j // 4), al(128 * (j % 4), 128)) for j in steps]

    def tile_at(first, at):
        row, col = places[at]
        return pl.ds(al(first + row, 8), 8), pl.ds(col, 128)

    waves = ((range(EARLY, 8), 1), (range(EARLY), 5))
    for slots, sem in waves:
        for k in (4, 3, 5, 2, 6, 1, 7):
            t, q, _ = plane_peer(k, 1)
            for at in slots:
                src = panel.at[tile_at(16 * q, at)]
                remote(src, came_a.at[p, at], reduce_sem.at[0], reduce_sem.at[sem], (t, ti)).start()
    for at in range(8):
        rows, cols = tile_at(16 * p, at)
        came_a[p, at] = panel[rows, cols]

    local_pair.wait()
    mate_pair.wait_recv()
    pass_pair.wait_recv()
    row = place_ids(h, 0, 0, pair.shape)
    near[...] = jnp.where(row < size, pair[...].astype(F32), 0.0).astype(BF)
    which = lax.broadcasted_iota(jnp.int32, (128, 512), 0)
    wanted = jnp.where(which < 64, which + 64 * ti, which + (256 - 64) + 64 * ti)
    hot = jnp.where(lax.broadcasted_iota(jnp.int32, (128, 512), 1) == wanted, 1.0, 0.0).astype(BF)
    u = dot_nt(hot, near[...]).astype(BF)
    wide[pl.ds(0, 128), :] = first_step(dot(u, xh[...]) + dot(u, xl[...]))

    for slots, sem in waves:
        count = len(slots)
        span = pl.ds(slots[0], count)
        drain(came_a.at[pl.ds(0, PLANE - 1), span], reduce_sem.at[sem])
        total = came_a[0, span]
        for q in range(1, PLANE):
            total = total + came_a[q, span]
        piece[span] = total
        for at in sorted(slots, key=lambda at: -min(COMES[at], 8 - COMES[at])):
            for one in range(2):
                to = 2 * steps[at] + one
                if at == 0:
                    to = z + 1 - 2 * lax.rem(z, 2)
                if at or one:
                    device = (to * PLANE + p, ti)
                    remote(piece.at[at], came_z.at[z], reduce_sem.at[2], reduce_sem.at[3], device).start()
    came_z[z] = piece[0]
    others_a = came_a.at[pl.ds(0, PLANE - 1)]
    cross_s = copy(start_hbm.at[:, near_cols], start_f.at[my_start, near_cols], cross, 4)
    mate_s = copy(start_hbm, start_f.at[my_start], mate, 4)

    v = wide[pl.ds(0, 128), :]
    w = product(product(v, kh[...], kl[...]), xh[...], xl[...])
    y_high, y_low = split(2.0 * v - first_step(w))
    to_near = dot(y_high, near[...]) + dot(y_low, near[...])
    to_glob = dot(y_high, g_perm[...]) + dot(y_low, g_perm[...])
    nxt[:, pl.ds(0, 256)] = to_near[0:64, 0:256]
    nxt[:, pl.ds(256, 512)] = to_glob[0:64, :]
    next_copy = copy(nxt, nxt_came, before, 5)
    off_out[...] = to_near[0:64, 256:512]
    diag_out[...] = to_near[64:128, 256:512]
    cross_out[...] = to_glob[64:128, :]
    local_base.wait()
    wide[...] = first_step(xh[mine, :].astype(F32) + xl[mine, :].astype(F32))

    others_z = came_z.at[pl.ds(0, z_count - 1)]
    drain(others_z, reduce_sem.at[3])
    total = came_z[0]
    for q in range(1, z_count):
        total = total + came_z[q]
    tile_rows, tile_cols = tile_at(16 * p, 0)
    own_piece = PLANE * ti + p
    tiles[own_piece, 0] = total + base[tile_rows, tile_cols]
    for k in sorted(range(2, z_count, 2), key=lambda k: -min(k, z_count - k)):
        at = COMES.index((z_count - k) // 2)
        late = 1 if at >= EARLY else 0
        here = tiles.at[own_piece, 0]
        remote(here, tiles.at[own_piece, at], reduce_sem.at[4], reduce_sem.at[9 + late], z_device(k)).start()

    def piece_of(hh, cc, q, wave):
        return tiles.at[PLANE * (2 * hh + cc) + q, pl.ds(0, EARLY) if wave == 0 else pl.ds(EARLY, 8 - EARLY)]

    order = (12, 11, 13, 10, 14, 4, 9, 15, 3, 5, 2, 6, 8, 1, 7)

    def spread(wave):
        here = piece_of(h, c, p, wave)
        came = []
        for k in order:
            made = remote(here, here, reduce_sem.at[6], recv_p.at[16 * wave + k], plane_device(k))
            made.start()
            came.append((k, made))
        remote(here, here, reduce_sem.at[7], reduce_sem.at[8 + 3 * wave], mate).start()
        return came

    def hand_over(came, wave):
        for k, made in came:
            made.wait_recv()
            _, q, hh = plane_peer(k, -1)
            ref = piece_of(hh, c, q, wave)
            remote(ref, ref, reduce_sem.at[7], reduce_sem.at[8 + 3 * wave], mate).start()

    v = wide[...]
    w = product(product(v, kh[...], kl[...]), xh[...], xl[...])
    drain(came_z.at[pl.ds(0, EARLY - 1)], reduce_sem.at[9])
    first_wave = spread(0)
    wide[...] = 2.0 * v - first_step(w)
    pass_s = hand_on(cross_s, start_f.at[cross_start, far_cols], 4)
    drain(came_z.at[pl.ds(0, 8 - EARLY)], reduce_sem.at[10])
    second_wave = spread(1)

    wide_high, wide_low = split(wide[...])
    yg = dot(wide_high, g_perm[...]) + dot(wide_low, g_perm[...])
    local_s.wait()
    mate_s.wait_recv()
    pass_s.wait_recv()
    start_f[far_cols, near_cols] = start_f[near_cols, far_cols].T
    s_high[...], s_low[...] = split(start_f[...])
    w_out[...] = product(yg, s_high[...], s_low[...])

    def lay_out(cc, slots):
        def body(i, carry):
            q = PLANE * (2 * (i // PLANE) + cc) + lax.rem(i, PLANE)
            for at in slots:
                rows, cols = tile_at(16 * q, at)
                schur[rows, cols] = tiles[q, at]
            return carry

        lax.fori_loop(0, 2 * PLANE, body, 0)

    hand_over(first_wave, 0)
    lay_out(c, range(EARLY))
    hand_over(second_wave, 1)
    lay_out(c, range(EARLY, 8))
    inner_out[...] = half_inner(c, w_out, schur)
    next_copy.wait_recv()
    last = jnp.where(tm == blocks - 1, 0.0, 1.0).astype(F32)
    diag_out[...] += nxt_came[:, pl.ds(0, 256)] * last
    cross_out[...] += nxt_came[:, pl.ds(256, 512)] * last
    others_p = schur.at[pl.ds(0, 16 * (2 * PLANE - 1))]
    everything = schur.at[pl.ds(0, 32 * PLANE)]
    drain(tiles.at[pl.ds(0, 2 * PLANE), pl.ds(0, EARLY)], reduce_sem.at[8])
    lay_out(1 - c, range(EARLY))
    drain(tiles.at[pl.ds(0, 2 * PLANE), pl.ds(EARLY, 8 - EARLY)], reduce_sem.at[11])
    lay_out(1 - c, range(EARLY, 8))

    for group in range(4):
        drain(rows_x.at[pl.ds(0, 256)], send_sem.at[group])
    drain(start_f.at[pl.ds(0, 256)], send_sem.at[4])
    next_copy.wait_send()
    drain(others_a, reduce_sem.at[0])
    drain(others_z, reduce_sem.at[2])
    drain(came_z.at[pl.ds(0, z_count // 2 - 1)], reduce_sem.at[4])
    drain(others_p, reduce_sem.at[6])
    drain(everything, reduce_sem.at[7])


def half_inner(which, w, schur):
    first = pl.ds(al(128 * which, 128), 128)
    second = pl.ds(al(256 + 128 * which, 128), 128)
    t_high, t_low = split(jnp.concatenate([schur[first, :], schur[second, :]], axis=0))
    return product(jnp.concatenate([w[:, first], w[:, second]], axis=1), t_high, t_low)


def finish_kernel(
    diag, off, cross, schur, w, inner, s_high, s_low,
    diag_out, off_out, cross_out, schur_out, back_out,
    back, sem,
):
    mine = pl.ds(al(128 * lax.axis_index("tile"), 128), 128)
    pairs = ((diag, diag_out), (off, off_out), (cross, cross_out), (schur.at[mine], schur_out))
    copies = [pltpu.make_async_copy(a, b, sem.at[i]) for i, (a, b) in enumerate(pairs)]
    for made in copies:
        made.start()
    ti = lax.axis_index("tile")
    whole = inner[...] + half_inner(1 - lax.rem(ti, 2), w, schur)
    for i in range(2):
        rows = pl.ds(96 * i, 96)
        back[rows, :] = 2.0 * w[rows, :] - product(whole[96 * i : 96 * (i + 1)], s_high[...], s_low[...])
        made = pltpu.make_async_copy(back.at[rows], back_out.at[rows], sem.at[4 + i])
        made.start()
        copies.append(made)
    for made in copies:
        made.wait()


VM = pl.BlockSpec(memory_space=pltpu.VMEM)
SM = pl.BlockSpec(memory_space=pltpu.SMEM)
ANY = pl.BlockSpec(memory_space=pl.ANY)
HBM = pl.BlockSpec(memory_space=pltpu.HBM)
DMA = pltpu.SemaphoreType.DMA


def shards(operator, initial, block_sizes, link_index, link_pair, link_global, schur_base, schur_start):
    order = operator.shape[2]
    z_count = lax.axis_size("tm") // PLANE
    out = pl.pallas_call(
        functools.partial(block_kernel, z_count),
        out_shape=[
            pltpu.VMEM((64, 256), F32),
            pltpu.VMEM((64, 256), F32),
            pltpu.VMEM((64, 512), F32),
            pltpu.VMEM((512, 512), F32),
            pltpu.VMEM((ROWS, 512), F32),
            pltpu.VMEM((ROWS, 512), F32),
            pltpu.VMEM((512, 512), BF),
            pltpu.VMEM((512, 512), BF),
        ],
        in_specs=[SM] + [HBM] * 7,
        out_specs=[VM] * 8,
        scratch_shapes=[pltpu.VMEM((order, order), BF)] * 4
        + [pltpu.VMEM((HALF, order), F32)] * 2
        + [pltpu.VMEM((HALF, HALF), F32)] * 2
        + [
            pltpu.VMEM((order, 512), BF),
            pltpu.VMEM((order, 512), BF),
            pltpu.VMEM((1, 512), jnp.int32),
            pltpu.VMEM((128, 512), F32),
            pltpu.VMEM((128, 512), F32),
            pltpu.VMEM((PLANE, 8, 8, 128), F32),
            pltpu.VMEM((8, 8, 128), F32),
            pltpu.VMEM((z_count, 8, 128), F32),
            pltpu.VMEM((4 * PLANE, 8, 8, 128), F32),
            pltpu.VMEM((order, 512), BF),
            pltpu.VMEM((order, 512), BF),
            pltpu.VMEM((64, order), F32),
            pltpu.VMEM((64, order), F32),
            pltpu.VMEM((512, 512), F32),
            pltpu.VMEM((ROWS, order), F32),
            DMA((7,)),
            DMA((6,)),
            DMA((22,)),
            DMA((4 * PLANE,)),
            DMA((12,)),
            pltpu.SemaphoreType.REGULAR((6,)),
        ],
        compiler_params=pltpu.CompilerParams(collective_id=0, has_side_effects=True, vmem_limit_bytes=GRANT),
        name="block_step",
    )(
        block_sizes,
        *(
            pltpu.with_memory_space_constraint(array, pltpu.HBM)
            for array in (
                operator[0], initial[0], link_global[0], link_pair[0], link_index, schur_base, schur_start
            )
        ),
    )
    diag, off, cross, schur, back = pl.pallas_call(
        finish_kernel,
        out_shape=[
            jax.ShapeDtypeStruct((64, 256), F32),
            jax.ShapeDtypeStruct((64, 256), F32),
            jax.ShapeDtypeStruct((64, 512), F32),
            jax.ShapeDtypeStruct((128, 512), F32),
            jax.ShapeDtypeStruct((ROWS, 512), F32),
        ],
        in_specs=[VM] * 8,
        out_specs=[ANY] * 5,
        scratch_shapes=[pltpu.VMEM((ROWS, 512), F32), DMA((6,))],
        compiler_params=pltpu.CompilerParams(vmem_limit_bytes=GRANT),
        name="finish",
    )(*out)
    return diag[None], off[None], cross[None], schur, back[None]


def solution(mesh):
    return jax.shard_map(
        shards,
        mesh=mesh,
        in_specs=(
            P("tm", "tile", None),
            P("tm", "tile", None),
            P("tm"),
            P("tm", None),
            P("tm", "tile", None),
            P("tm", "tile", None),
            P("tile", None),
            P("tile", None),
        ),
        out_specs=(
            P("tm", "tile", None),
            P("tm", "tile", None),
            P("tm", "tile", None),
            P("tile", None),
            P("tm", "tile", None),
        ),
        check_vma=False,
    )
```
